32 devices in a mesh: blk: 8 (over z, y), grp: 4 (over x, core).
Axes of the slice: x: 2, y: 2, z: 4, core: 2. Of those that a mesh axis runs over, the one named last changes fastest.
Arguments:
- spectra: bfloat16 [4, 2048, 2, 16, 256], P('grp', 'blk'), may hold values from -6 to 6
- detector_valid: int32 [4, 2048], P('grp', 'blk'), may hold values 0 or 1
Outputs:
- coherence: float32 [2, 4, 2048, 8192], P(None, None, 'blk', 'grp')
The draws below stay inside these ranges and needn't reach their ends.
All inputs are finite; a program needn't handle non-finite values. No bound on the sum of `detector_valid` on one device may be relied on, other than what follows from the above.
Results may differ from the reference program's by a relative error of at most 0.0003.
Values may be sent and summed in bfloat16 or wider, within the bound.
No kernel may reach another device: no remote copies, remote signals or barrier semaphores. Data moves between devices by JAX's collectives and lax.ppermute only.
A program may use at most 128 MiB of HBM per device.

```python
import math
import jax
import jax.numpy as jnp
from jax import lax

DET = 8192
K = 256
BINS = 16
GBLK = 2048
N_GRP = 4


def place_ends(entries, own_key, low, high):
    longest = entries.shape.index(max(entries.shape))
    spots = []
    for shift in (0, 1):
        where = [jax.random.randint(jax.random.fold_in(own_key, axis), (), 0, length) for axis, length in enumerate(entries.shape)]
        where[longest] = (where[longest] + shift) % entries.shape[longest]
        spots.append(tuple(where))
    return entries.at[spots[0]].set(low).at[spots[1]].set(high)


def shard_levels(own_key, extent, split, least, top_value):
    def one(axis_at, blocks):
        steps = jax.random.uniform(jax.random.fold_in(jax.random.fold_in(own_key, 6), axis_at), (blocks,), jnp.float32, least / len(split), top_value / len(split))
        return jnp.repeat(jnp.exp(steps), extent[axis_at] // blocks).reshape((-1,) + (1,) * (len(extent) - axis_at - 1))

    level = one(*split[0])
    for cut in split[1:]:
        level = level * one(*cut)
    return level


def gaussian(stream_key, dims, spread, bound, split=(), held_as=jnp.bfloat16):
    drawn = spread * jax.random.normal(stream_key, dims, jnp.float32)
    if split:
        drawn = drawn * shard_levels(stream_key, dims, split, -0.22, 0.18)
    return jnp.clip(drawn, -bound, bound).astype(held_as)


def setup_inputs(seed: int = 0) -> dict:
    streams_of = jax.random.split(jax.random.key(seed), 3)
    return {
        "spectra": gaussian(streams_of[0], (N_GRP, GBLK, 2, BINS, K), 1.0, 6.0, ((0, 4), (1, 8))),
        "detector_valid": place_ends((jax.random.randint(streams_of[1], (N_GRP, GBLK), 0, 8) < 7).astype(jnp.int32), jax.random.fold_in(streams_of[1], 1), 0, 1),
    }


def reference(spectra, detector_valid):
    half_width = BINS * K
    flattened = spectra.reshape(DET, 2 * half_width).astype(jnp.float32)
    power_mean = lax.optimization_barrier(jnp.mean(flattened * flattened, axis=1)) + 1e-06
    factor = detector_valid.reshape(DET).astype(jnp.float32) * lax.rsqrt(power_mean)
    rotated = jnp.concatenate([-flattened[:, half_width:], flattened[:, :half_width]], axis=1)
    scale_coef = 0.5 / math.sqrt(half_width)
    block_rows = min(DET, 512)
    row_blocks = flattened.reshape(DET // block_rows, block_rows, 2 * half_width)
    factor_blocks = factor.reshape(DET // block_rows, block_rows)

    def one_block(inputs):
        row_vals, row_factor = inputs
        real_part = jnp.dot(row_vals, flattened.T, precision=lax.Precision.HIGHEST, preferred_element_type=jnp.float32)
        imag_part = jnp.dot(row_vals, rotated.T, precision=lax.Precision.HIGHEST, preferred_element_type=jnp.float32)
        scaling = (row_factor * scale_coef)[:, None] * factor[None, :]
        return jnp.stack([real_part * scaling, imag_part * scaling])
    stacked = lax.map(one_block, (row_blocks, factor_blocks))
    result = jnp.transpose(stacked, (1, 0, 2, 3)).reshape(2, DET, DET)
    return result.reshape(2, N_GRP, GBLK, DET)
```

```python
import functools
import math

import jax
import jax.numpy as jnp
from jax import lax
from jax.experimental import pallas as pl
from jax.experimental.pallas import tpu as pltpu
from jax.sharding import PartitionSpec as P

NT = (((1,), (1,)), ((), ()))


def tile_of(size, most):
    tile = 1
    while tile * 2 <= most and size % (tile * 2) == 0:
        tile *= 2
    return tile


def factors(flattened, flag_vals):
    widened = flattened.astype(jnp.float32)
    power_mean = jnp.mean(widened * widened, axis=1) + 1e-06
    return flag_vals.astype(jnp.float32) * lax.rsqrt(power_mean)


def tile_body(pieces, steps, slot_ref, real_ref, imag_ref, *refs):
    col_real, col_imag = refs[:pieces], refs[pieces : 2 * pieces]
    row_factor, col_factor = refs[2 * pieces : 2 * pieces + 2]
    out_ref, total = refs[-2:]
    step = pl.program_id(1)
    rows_real, rows_imag = real_ref[...], imag_ref[...]
    cols_real = jnp.concatenate([ref[...] for ref in col_real], axis=0)
    cols_imag = jnp.concatenate([ref[...] for ref in col_imag], axis=0)

    def dot(left, right):
        return lax.dot_general(left, right, NT, preferred_element_type=jnp.float32)

    real = dot(rows_real, cols_real) + dot(rows_imag, cols_imag)
    imag = dot(rows_imag, cols_real) - dot(rows_real, cols_imag)

    @pl.when(step == 0)
    def _():
        total[0] = real
        total[1] = imag

    @pl.when(step > 0)
    def _():
        total[0] += real
        total[1] += imag

    @pl.when(step == steps - 1)
    def _():
        scaling = row_factor[...] * col_factor[...]
        out_ref[0] = total[0] * scaling
        out_ref[1] = total[1] * scaling


def put_tile(output_tile, rows, pieces, slot, row_factor, col_factor):
    row_count, full_width = rows.shape
    half_width = full_width // 2
    shard_rows = sum(piece.shape[0] for piece in pieces)
    depth = tile_of(half_width, 1024)
    high = tile_of(row_count, 1024)
    steps = half_width // depth
    count = len(pieces)
    specs = [
        pl.BlockSpec((high, depth), lambda i, k, s: (i, k)),
        pl.BlockSpec((high, depth), lambda i, k, s: (i, k + steps)),
    ]
    specs += [pl.BlockSpec((p.shape[0], depth), lambda i, k, s: (0, k)) for p in pieces]
    specs += [pl.BlockSpec((p.shape[0], depth), lambda i, k, s: (0, k + steps)) for p in pieces]
    specs += [
        pl.BlockSpec((high, 1), lambda i, k, s: (i, 0)),
        pl.BlockSpec((1, shard_rows), lambda i, k, s: (0, s[0])),
    ]
    operands = [slot.reshape(1), rows, rows, *pieces, *pieces, row_factor, col_factor]
    aliases = {}
    if output_tile is not None:
        specs.append(pl.BlockSpec(memory_space=pl.ANY))
        aliases = {len(operands): 0}
        operands.append(output_tile)
    return pl.pallas_call(
        functools.partial(tile_body, count, steps),
        grid_spec=pltpu.PrefetchScalarGridSpec(
            num_scalar_prefetch=1,
            grid=(row_count // high, steps),
            in_specs=specs,
            out_specs=pl.BlockSpec((2, high, shard_rows), lambda i, k, s: (0, i, s[0])),
            scratch_shapes=[pltpu.VMEM((2, high, shard_rows), jnp.float32)],
        ),
        out_shape=jax.ShapeDtypeStruct((2, row_count, col_factor.shape[1]), jnp.float32),
        input_output_aliases=aliases,
        cost_estimate=pl.CostEstimate(
            flops=4 * row_count * shard_rows * full_width,
            bytes_accessed=2 * full_width * (row_count + shard_rows) + 8 * row_count * shard_rows,
            transcendentals=0,
        ),
        compiler_params=pltpu.CompilerParams(dimension_semantics=("arbitrary", "arbitrary")),
    )(*operands)


def cycle_of(count):
    return list(range(0, count, 2)) + list(range(count - 1, 0, -2))


def gathered(flattened, own_factor, scale_coef):
    half_width = flattened.shape[1] // 2
    rows = lax.all_gather(flattened, "grp", axis=0, tiled=True)
    cols = lax.all_gather(flattened, "blk", axis=0, tiled=True)
    row_factor = lax.all_gather(own_factor, "grp", axis=0, tiled=True) * scale_coef
    col_factor = lax.all_gather(own_factor, "blk", axis=0, tiled=True)
    rotated = jnp.concatenate([-cols[:, half_width:], cols[:, :half_width]], axis=1)
    scaling = row_factor[:, None] * col_factor[None, :]
    parts = [
        lax.dot_general(rows, right, NT, preferred_element_type=jnp.float32) * scaling
        for right in (cols, rotated)
    ]
    return jnp.stack(parts)


def shards(spectra, detector_valid):
    shard_rows = spectra.shape[1]
    half_width = spectra.shape[3] * spectra.shape[4]
    cycle_size = lax.axis_size("blk")
    group_size = lax.axis_size("grp")
    scale_coef = 0.5 / math.sqrt(half_width)
    flattened = spectra.reshape(shard_rows, 2 * half_width)
    own_factor = factors(flattened, detector_valid.reshape(shard_rows))
    shape = (2, group_size, shard_rows, cycle_size * shard_rows)
    if shard_rows % 128 or half_width % 128 or cycle_size % 2 or cycle_size < 4:
        return gathered(flattened, own_factor, scale_coef).reshape(shape)

    ring = cycle_of(cycle_size)
    onward = [(ring[i], ring[(i + 1) % cycle_size]) for i in range(cycle_size)]
    backward = [(there, here) for here, there in onward]
    place = jnp.array([ring.index(i) for i in range(cycle_size)], jnp.int32)[lax.axis_index("blk")]
    at = jnp.array(ring + ring, jnp.int32)

    rows = lax.all_gather(flattened, "grp", axis=0, tiled=True)
    row_factor = lax.all_gather(own_factor, "grp", axis=0, tiled=True) * scale_coef
    col_factor = lax.all_gather(own_factor, "blk", axis=0, tiled=True)

    def put(output_tile, pieces, offset):
        slot = at[place + offset % cycle_size]
        return put_tile(output_tile, rows, pieces, slot, row_factor[:, None], col_factor[None, :])

    half = shard_rows // 2
    last = cycle_size // 2
    low, high = flattened, flattened
    waiting = [((flattened,), 0)]
    output_tile = None
    for offset in range(1, last + 1):
        if offset == last:
            low, high = low[:half], high[half:]
        low = lax.ppermute(low, "blk", onward)
        high = lax.ppermute(high, "blk", backward)
        if offset > 1:
            for pieces, behind in waiting:
                output_tile = put(output_tile, pieces, behind)
            waiting = []
        if offset == last:
            output_tile = put(output_tile, (low, high), last)
        else:
            waiting += [((low,), -offset), ((high,), offset)]
            if offset > 1:
                low, high, output_tile = lax.optimization_barrier((low, high, output_tile))
    return output_tile.reshape(shape)


def solution(mesh):
    return jax.shard_map(
        shards,
        mesh=mesh,
        in_specs=(P("grp", "blk", None, None, None), P("grp", "blk")),
        out_specs=P(None, None, "blk", "grp"),
        check_vma=False,
    )
```

```python
import functools
import math

import jax
import jax.numpy as jnp
from jax import lax
from jax.experimental import pallas as pl
from jax.experimental.pallas import tpu as pltpu
from jax.sharding import PartitionSpec as P


NT = (((1,), (1,)), ((), ()))
LANES = 128
FLOOR = 1e-30


def tile_of(size, most):
    tile = 1
    while tile * 2 <= most and size % (tile * 2) == 0:
        tile *= 2
    return tile


def exchange(value, axis, pairs):
    return lax.ppermute(value, axis, pairs)


def tied(*values):
    return lax.optimization_barrier(values)


def split_in_three(value):
    parts = []
    for _ in range(2):
        part = value.astype(jnp.bfloat16).astype(jnp.float32)
        parts.append(part)
        value = value - part
    return parts + [value]


def laid_out_body(spectra_ref, flags_ref, out_ref):
    high, parts, bins, taps = spectra_ref.shape
    half_width = bins * taps
    power = jnp.zeros((high, 1), jnp.float32)
    for part in range(parts):
        flat = spectra_ref[:, part].reshape(high, half_width)
        out_ref[:, part * half_width : (part + 1) * half_width] = flat
        widened = flat.astype(jnp.float32)
        power = power + jnp.sum(widened * widened, axis=1, keepdims=True)
    power_mean = power / (parts * half_width)
    factor = flags_ref[...].astype(jnp.float32) * lax.rsqrt(power_mean + 1e-06)
    norm = lax.rsqrt(jnp.maximum(power_mean, FLOOR))
    lane = lax.broadcasted_iota(jnp.int32, (high, LANES), 1)
    marks = jnp.zeros((high, LANES), jnp.float32)
    for index, value in enumerate(split_in_three(factor) + split_in_three(norm)):
        marks = jnp.where(lane == index, value, marks)
    out_ref[:, parts * half_width :] = marks.astype(jnp.bfloat16)


def laid_out(spectra, flags):
    rows, parts, bins, taps = spectra.shape
    width = parts * bins * taps + LANES
    high = tile_of(rows, 64)
    return pl.pallas_call(
        laid_out_body,
        grid=(rows // high,),
        in_specs=[
            pl.BlockSpec((high, parts, bins, taps), lambda i: (i, 0, 0, 0)),
            pl.BlockSpec((high, 1), lambda i: (i, 0)),
        ],
        out_specs=pl.BlockSpec((high, width), lambda i: (i, 0)),
        out_shape=jax.ShapeDtypeStruct((rows, width), spectra.dtype),
    )(spectra, flags.reshape(rows, 1))


def products_body(sizes, scale_coef, raw, plan_ref, *refs):
    row_total, shapes, kept, units, steps = sizes
    refs = list(refs)

    def take(count):
        taken = refs[:count]
        del refs[:count]
        return taken

    rows_real, rows_imag, row_marks = take(row_total), take(row_total), take(row_total)
    columns = [(take(len(s)), take(len(s)), take(len(s))) for s in shapes]
    placed = [take(2) for _ in range(kept)]
    total, right = refs[-2:]
    outs = refs[-4:-2] if raw else refs[-3:-2]
    out_ref = outs[0]
    unit, step = pl.program_id(0), pl.program_id(1)
    chosen = plan_ref[unit]
    depth = rows_real[0].shape[1]
    shard_rows = right.shape[0] // 2

    def marks_of(values, first):
        return (values[first + 2] + values[first + 1]) + values[first]

    def column_marks(marks):
        flipped = jnp.concatenate([m[...] for m in marks], axis=0).astype(jnp.float32).T
        rows = [flipped[i : i + 1] for i in range(6)]
        return marks_of(rows, 0), marks_of(rows, 3)

    def marks_of_rows(ref):
        values = ref[...].astype(jnp.float32)
        values = [values[:, i : i + 1] for i in range(6)]
        return marks_of(values, 0), marks_of(values, 3)

    for index, (reals, imags, _) in enumerate(columns):

        @pl.when(chosen == index)
        def _():
            at = 0
            for real_ref, imag_ref in zip(reals, imags):
                end = at + real_ref.shape[0]
                right[at:end, :depth] = real_ref[...]
                right[at:end, depth:] = imag_ref[...]
                right[shard_rows + at : shard_rows + end, :depth] = -imag_ref[...]
                right[shard_rows + at : shard_rows + end, depth:] = real_ref[...]
                at = end

    @pl.when(jnp.logical_and(chosen >= 0, chosen < len(columns)))
    def _():
        left = jnp.concatenate(
            [
                jnp.concatenate([ref[...] for ref in rows_real], axis=0),
                jnp.concatenate([ref[...] for ref in rows_imag], axis=0),
            ],
            axis=1,
        )
        product = lax.dot_general(left, right[...], NT, preferred_element_type=jnp.float32)

        @pl.when(step == 0)
        def _():
            total[...] = product

        @pl.when(step > 0)
        def _():
            total[...] += product

    for index, (_, _, marks) in enumerate(columns):

        @pl.when(jnp.logical_and(chosen == index, step == steps - 1))
        def _():
            col_factor, col_norm = column_marks(marks)
            if raw:
                outs[1][...] = jnp.broadcast_to(col_factor / col_norm, outs[1].shape)
            for row in range(row_total):
                row_factor, row_norm = marks_of_rows(row_marks[row])
                scaling = row_norm * col_norm if raw else (row_factor * scale_coef) * col_factor
                group = plan_ref[2 * units + row]
                held = slice(row * shard_rows, (row + 1) * shard_rows)
                out_ref[0, group] = total[held, :shard_rows] * scaling
                out_ref[1, group] = total[held, shard_rows:] * scaling

    for index, (block_ref, ratio_ref) in enumerate(placed):

        @pl.when(jnp.logical_and(chosen == len(columns) + index, step == steps - 1))
        def _():
            ratio = ratio_ref[0:1]
            for row in range(row_total):
                row_factor, row_norm = marks_of_rows(row_marks[row])
                scaling = (row_factor / row_norm * scale_coef) * ratio
                group = plan_ref[2 * units + row]
                out_ref[0, group] = block_ref[0, group] * scaling
                out_ref[1, group] = block_ref[1, group] * scaling


def products(out, rows, columns, placed, choice, slots, groups, blocks, scale_coef, raw=False):
    shard_rows, width = rows[0].shape
    half_width = (width - LANES) // 2
    depth = tile_of(half_width, 1024)
    steps = half_width // depth
    units = len(choice)
    count = len(rows)
    last = (width - LANES) // LANES

    def fixed(row_height, first):
        return pl.BlockSpec((row_height, depth), lambda i, k, s: (0, k + first))

    def picked(row_height, index, first):
        return pl.BlockSpec(
            (row_height, depth), lambda i, k, s: (0, jnp.where(s[i] == index, k, 0) + first)
        )

    def marks(row_height):
        return pl.BlockSpec((row_height, LANES), lambda i, k, s: (0, last))

    specs = [fixed(shard_rows, 0)] * count + [fixed(shard_rows, steps)] * count
    specs += [marks(shard_rows)] * count
    operands = list(rows) * 3
    for index, pieces in enumerate(columns):
        specs += [picked(p.shape[0], index, 0) for p in pieces]
        specs += [picked(p.shape[0], index, steps) for p in pieces]
        specs += [marks(p.shape[0]) for p in pieces]
        operands += list(pieces) * 3
    block = (2, count, shard_rows, shard_rows)
    for pair in placed:
        specs.append(pl.BlockSpec(block, lambda i, k, s: (0, 0, 0, 0)))
        specs.append(pl.BlockSpec(pair[1].shape, lambda i, k, s: (0, 0)))
        operands += list(pair)
    plan = jnp.stack(list(choice) + list(slots) + list(groups)).astype(jnp.int32)
    aliases = {}
    if out is not None:
        specs.append(pl.BlockSpec(memory_space=pl.ANY))
        aliases = {1 + len(operands): 0}
        operands.append(out)
    whole = (2, count, shard_rows, shard_rows * (1 if raw else blocks))
    out_shape = [jax.ShapeDtypeStruct(whole, jnp.float32)]
    out_specs = [pl.BlockSpec(block, lambda i, k, s: (0, 0, 0, s[units + i]))]
    if raw:
        out_shape.append(jax.ShapeDtypeStruct((8, shard_rows), jnp.float32))
        out_specs.append(pl.BlockSpec((8, shard_rows), lambda i, k, s: (0, 0)))
    sizes = (count, [[p.shape[0] for p in c] for c in columns], len(placed), units, steps)
    given = pl.pallas_call(
        functools.partial(products_body, sizes, scale_coef, raw),
        grid_spec=pltpu.PrefetchScalarGridSpec(
            num_scalar_prefetch=1,
            grid=(units, steps),
            in_specs=specs,
            out_specs=out_specs,
            scratch_shapes=[
                pltpu.VMEM((count * shard_rows, 2 * shard_rows), jnp.float32),
                pltpu.VMEM((2 * shard_rows, 2 * depth), rows[0].dtype),
            ],
        ),
        out_shape=out_shape,
        input_output_aliases=aliases,
        cost_estimate=pl.CostEstimate(
            flops=8 * units * count * shard_rows * shard_rows * half_width,
            bytes_accessed=4 * units * half_width * (count + 1) * shard_rows,
            transcendentals=0,
        ),
        compiler_params=pltpu.CompilerParams(
            dimension_semantics=("arbitrary", "arbitrary"), vmem_limit_bytes=60 * 2**20
        ),
    )(plan, *operands)
    return given if raw else given[0]


def gathered(spectra, detector_valid, scale_coef):
    shard_rows = spectra.shape[1]
    half_width = spectra.shape[3] * spectra.shape[4]
    flattened = spectra.reshape(shard_rows, 2 * half_width)
    widened = flattened.astype(jnp.float32)
    power_mean = jnp.mean(widened * widened, axis=1) + 1e-06
    own_factor = detector_valid.reshape(shard_rows).astype(jnp.float32) * lax.rsqrt(power_mean)
    rows = lax.all_gather(flattened, "grp", axis=0, tiled=True)
    cols = lax.all_gather(flattened, "blk", axis=0, tiled=True)
    row_factor = lax.all_gather(own_factor, "grp", axis=0, tiled=True) * scale_coef
    col_factor = lax.all_gather(own_factor, "blk", axis=0, tiled=True)
    rotated = jnp.concatenate([-cols[:, half_width:], cols[:, :half_width]], axis=1)
    scaling = row_factor[:, None] * col_factor[None, :]
    parts = [
        lax.dot_general(rows, right, NT, preferred_element_type=jnp.float32) * scaling
        for right in (cols, rotated)
    ]
    return jnp.stack(parts)


def shards(spectra, detector_valid):
    shard_rows = spectra.shape[1]
    half_width = spectra.shape[3] * spectra.shape[4]
    blocks = lax.axis_size("blk")
    group_size = lax.axis_size("grp")
    scale_coef = 0.5 / math.sqrt(half_width)
    shape = (2, group_size, shard_rows, blocks * shard_rows)
    fits = shard_rows % 256 == 0 and half_width % 256 == 0 and group_size & (group_size - 1) == 0
    if blocks != 8 or not fits:
        return gathered(spectra, detector_valid, scale_coef).reshape(shape)

    devices = range(blocks)
    inner = [b for b in devices if 0 < b // 2 < blocks // 2 - 1]
    ends = [b for b in devices if b not in inner]
    me = lax.axis_index("blk")
    mine = lax.axis_index("grp")
    is_end = jnp.logical_or(me // 2 == 0, me // 2 == blocks // 2 - 1)

    def swap(value, among, by):
        return exchange(value, "blk", [(b, b ^ by) for b in among])

    def spread(value, by):
        return exchange(value, "grp", [(g, g ^ by) for g in range(group_size)])

    groups = [mine]
    by = group_size // 2
    while by:
        groups += [g ^ by for g in groups]
        by //= 2

    def over_groups(value):
        arrays, by = [value], group_size // 2
        while by:
            arrays += [spread(array, by) for array in arrays]
            by //= 2
        return arrays

    def either(inner_value, end_value):
        return jnp.where(is_end, end_value, inner_value)

    def put(out, rows, columns, placed, units):
        choice = [either(m, e) for m, e, _, _ in units]
        slots = [either(me ^ m, me ^ e) for _, _, m, e in units]
        return products(
            out, rows, columns, placed, choice, slots, groups, blocks, scale_coef
        )

    own = laid_out(spectra[0], detector_valid[0])
    near = swap(own, devices, 2)
    beside = swap(own, devices, 1)
    across = swap(own, inner, 6)
    rows = over_groups(own)

    across_beside = swap(across, inner, 1)
    near_beside = swap(near, ends, 1)
    end_beside = swap(beside, ends, 2)
    far_inner = swap(across, inner, 2)
    far_end = swap(near, inner, 6)
    client = over_groups(near)
    out = put(
        None,
        rows,
        [(own,), (near,), (beside,), (across,)],
        [],
        [(0, 0, 0, 0), (1, 1, 2, 2), (2, 2, 1, 1), (3, -1, 6, 5)],
    )

    far_end, end_beside, out = tied(far_end, end_beside, out)
    half = shard_rows // 2
    low = swap(far_end[:half], inner, 1)
    high = swap(end_beside[half:], inner, 6)

    def serve(columns):
        choice = [either(0, -1)]
        return products(
            None, client, [columns], [], choice, [me * 0], groups, blocks, scale_coef, raw=True
        )

    def deliver(block, ratio):
        return swap(block.astype(jnp.float16), inner, 2), swap(ratio, inner, 2)

    block_a, ratio_a = serve((across_beside,))
    sent_a = deliver(block_a, ratio_a)
    far_end, ratio_a = tied(far_end, ratio_a)
    block_b, ratio_b = serve((far_end,))
    sent_b = deliver(block_b, ratio_b)
    out, ratio_b = tied(out, ratio_b)
    out = put(out, rows, [(across_beside,), (near_beside,)], [], [(0, 1, 7, 3)])
    low, high, out = tied(low, high, out)
    block_c, ratio_c = serve((low, high))
    sent_c = deliver(block_c, ratio_c)
    out, ratio_c = tied(out, ratio_c)
    out = put(
        out,
        rows,
        [(end_beside,), (far_inner,), (far_end,)],
        [],
        [(0, 1, 3, 4), (2, -1, 4, 6)],
    )
    placed = [(block.astype(jnp.float32), ratio) for block, ratio in (sent_a, sent_b, sent_c)]
    out = put(
        out,
        rows,
        [(low, high)],
        placed,
        [(-1, 1, 5, 5), (-1, 2, 5, 6), (-1, 3, 5, 7), (0, -1, 5, 7)],
    )
    return out.reshape(shape)


def solution(mesh):
    return jax.shard_map(
        shards,
        mesh=mesh,
        in_specs=(P("grp", "blk", None, None, None), P("grp", "blk")),
        out_specs=P(None, None, "blk", "grp"),
        check_vma=False,
    )
```

```python
import functools
import math

import jax
import jax.numpy as jnp
from jax import lax
from jax.experimental import pallas as pl
from jax.experimental.pallas import tpu as pltpu
from jax.sharding import PartitionSpec as P


NT = (((1,), (1,)), ((), ()))
LANES = 128
FLOOR = 1e-30


def tile_of(size, most):
    tile = 1
    while tile * 2 <= most and size % (tile * 2) == 0:
        tile *= 2
    return tile


def tied(*values):
    return lax.optimization_barrier(values)


def split_in_three(value):
    parts = []
    for _ in range(2):
        part = value.astype(jnp.bfloat16).astype(jnp.float32)
        parts.append(part)
        value = value - part
    return parts + [value]


def laid_out_body(pieces, spectra_ref, flags_ref, *out_refs):
    high, parts, bins, taps = spectra_ref.shape
    per_piece = pl.num_programs(0) // pieces
    half_width = bins * taps

    def fill(out_ref):
        power = jnp.zeros((high, 1), jnp.float32)
        for part in range(parts):
            flat = spectra_ref[:, part].reshape(high, half_width)
            out_ref[:, part * half_width : (part + 1) * half_width] = flat
            widened = flat.astype(jnp.float32)
            power = power + jnp.sum(widened * widened, axis=1, keepdims=True)
        power_mean = power / (parts * half_width)
        factor = flags_ref[...].astype(jnp.float32) * lax.rsqrt(power_mean + 1e-06)
        norm = lax.rsqrt(jnp.maximum(power_mean, FLOOR))
        lane = lax.broadcasted_iota(jnp.int32, (high, LANES), 1)
        marks = jnp.zeros((high, LANES), jnp.float32)
        for index, value in enumerate(split_in_three(factor) + split_in_three(norm)):
            marks = jnp.where(lane == index, value, marks)
        out_ref[:, parts * half_width :] = marks.astype(jnp.bfloat16)

    for piece, out_ref in enumerate(out_refs):
        pl.when(pl.program_id(0) // per_piece == piece)(functools.partial(fill, out_ref))


def laid_out(spectra, flags, pieces):
    rows, parts, bins, taps = spectra.shape
    width = parts * bins * taps + LANES
    high = tile_of(rows // pieces, 64)
    per_piece = rows // pieces // high

    def place(piece):
        first = piece * per_piece
        return lambda i: (jnp.clip(i - first, 0, per_piece - 1), 0)

    return pl.pallas_call(
        functools.partial(laid_out_body, pieces),
        grid=(rows // high,),
        in_specs=[
            pl.BlockSpec((high, parts, bins, taps), lambda i: (i, 0, 0, 0)),
            pl.BlockSpec((high, 1), lambda i: (i, 0)),
        ],
        out_specs=[pl.BlockSpec((high, width), place(piece)) for piece in range(pieces)],
        out_shape=[jax.ShapeDtypeStruct((rows // pieces, width), spectra.dtype)] * pieces,
    )(spectra, flags.reshape(rows, 1))


def products_body(sizes, scale_coef, raw, plan_ref, *refs):
    row_total, at_once, shapes, units = sizes
    refs = list(refs)
    rows = refs[:row_total]
    columns, at = [], row_total
    for shape in shapes:
        columns.append(refs[at : at + len(shape)])
        at += len(shape)
    held, right, col_marks, row_sems, col_sems = refs[-5:]
    outs = refs[-7:-5] if raw else refs[-6:-5]
    out_ref = outs[0]
    unit, part = pl.program_id(0), pl.program_id(1)
    parts = row_total // at_once
    now = unit * parts + part
    shard_rows = held.shape[1] // at_once
    cols = right.shape[1] // 2
    half_width = right.shape[2] // 2

    def row_copy(index, row, slot):
        where = held.at[slot, pl.ds(row * shard_rows, shard_rows)]
        return pltpu.make_async_copy(rows[index], where, row_sems.at[slot, row])

    def start_rows(which, slot):
        for index in range(parts):

            @pl.when(which == index)
            def _():
                for row in range(at_once):
                    row_copy(index * at_once + row, row, slot).start()

    def col_copies(index, slot):
        copies, top = [], 0
        for number, piece in enumerate(columns[index]):
            high = piece.shape[0]
            real, imag = piece.at[:, pl.ds(0, half_width)], piece.at[:, pl.ds(half_width, half_width)]
            marks = piece.at[:, pl.ds(2 * half_width, LANES)]
            places = [
                (real, right.at[slot, pl.ds(top, high), pl.ds(0, half_width)]),
                (imag, right.at[slot, pl.ds(top, high), pl.ds(half_width, half_width)]),
                (real, right.at[slot, pl.ds(cols + top, high), pl.ds(half_width, half_width)]),
                (marks, col_marks.at[slot, pl.ds(top, high)]),
            ]
            for kind, (source, target) in enumerate(places):
                copies.append(
                    pltpu.make_async_copy(source, target, col_sems.at[slot, 4 * number + kind])
                )
            top += high
        return copies

    def for_cols(which, slot, wait):
        for index in range(len(columns)):

            @pl.when(plan_ref[which] == index)
            def _():
                for copy in col_copies(index, slot):
                    copy.wait() if wait else copy.start()

    slot, col_slot = lax.rem(now, 2), lax.rem(unit, 2)

    @pl.when(now == 0)
    def _():
        start_rows(0, 0)
        for_cols(0, 0, False)

    @pl.when(now + 1 < units * parts)
    def _():
        start_rows(lax.rem(part + 1, parts), lax.rem(now + 1, 2))

    @pl.when(jnp.logical_and(part == 0, unit + 1 < units))
    def _():
        for_cols(unit + 1, lax.rem(unit + 1, 2), False)

    @pl.when(part == 0)
    def _():
        for_cols(unit, col_slot, True)
        right[col_slot, cols:, :half_width] = -right[col_slot, :cols, half_width:]

    for row in range(at_once):
        row_copy(row, row, slot).wait()

    left = held[slot, :, : 2 * half_width]
    product = lax.dot_general(left, right[col_slot], NT, preferred_element_type=jnp.float32)

    def sums(values, axis):
        def one(first):
            take = [lax.slice_in_dim(values, i, i + 1, axis=axis) for i in range(first, first + 3)]
            return (take[2] + take[1]) + take[0]

        return one(0), one(3)

    col_factor, col_norm = sums(col_marks[col_slot].astype(jnp.float32).T, 0)
    for row in range(at_once):
        top = row * shard_rows
        marks = held[slot, pl.ds(top, shard_rows), pl.ds(2 * half_width, LANES)]
        row_factor, row_norm = sums(marks.astype(jnp.float32), 1)
        place = plan_ref[2 * units + parts + part * at_once + row]
        scaling = (row_factor * scale_coef) * col_factor
        if raw:
            bound = jnp.max(row_factor / row_norm, axis=0, keepdims=True)
            bound = bound * jnp.max(col_factor / col_norm, axis=1, keepdims=True)
            unit_size = jnp.maximum(bound * (2 * half_width * scale_coef), FLOOR) / 32768
            outs[1][place] = jnp.broadcast_to(unit_size, outs[1].shape[1:])
            scaling = scaling * (1 / unit_size)
        out_ref[0, place] = product[top : top + shard_rows, :cols] * scaling
        out_ref[1, place] = product[top : top + shard_rows, cols:] * scaling


def products(out, rows, columns, choice, slots, mine, blocks, scale_coef, raw=False):
    shard_rows, width = rows[0].shape
    half_width = (width - LANES) // 2
    units, count = len(choice), len(rows)
    at_once = 2 if units > 1 and count > 1 else 1
    parts = count // at_once
    cols = sum(piece.shape[0] for piece in columns[0])
    whole = pl.BlockSpec(memory_space=pl.ANY)
    operands = list(rows) + [piece for pieces in columns for piece in pieces]
    aliases = {}
    if out is not None:
        aliases = {1 + len(operands): 0}
        operands.append(out)
    groups = [mine ^ j for j in range(count)]
    plan = jnp.stack(
        list(choice)
        + list(slots)
        + [group // at_once for group in groups[::at_once]]
        + [group % at_once for group in groups]
    ).astype(jnp.int32)
    shape = (2, count, shard_rows, cols if raw else shard_rows * blocks)
    out_shape = [jax.ShapeDtypeStruct(shape, jnp.float32)]
    out_specs = [
        pl.BlockSpec(
            (2, at_once, shard_rows, cols),
            lambda i, j, s: (0, s[2 * units + j], 0, s[units + i]),
        )
    ]
    if raw:
        out_shape.append(jax.ShapeDtypeStruct((count, 8, LANES), jnp.float32))
        out_specs.append(
            pl.BlockSpec((at_once, 8, LANES), lambda i, j, s: (s[2 * units + j], 0, 0))
        )
    shapes = [[piece.shape[0] for piece in pieces] for pieces in columns]
    most = max(len(pieces) for pieces in columns)
    given = pl.pallas_call(
        functools.partial(products_body, (count, at_once, shapes, units), scale_coef, raw),
        grid_spec=pltpu.PrefetchScalarGridSpec(
            num_scalar_prefetch=1,
            grid=(units, parts),
            in_specs=[whole] * len(operands),
            out_specs=out_specs,
            scratch_shapes=[
                pltpu.VMEM((2, at_once * shard_rows, width), rows[0].dtype),
                pltpu.VMEM((2, 2 * cols, 2 * half_width), rows[0].dtype),
                pltpu.VMEM((2, cols, LANES), rows[0].dtype),
                pltpu.SemaphoreType.DMA((2, at_once)),
                pltpu.SemaphoreType.DMA((2, 4 * most)),
            ],
        ),
        out_shape=out_shape,
        input_output_aliases=aliases,
        cost_estimate=pl.CostEstimate(
            flops=8 * units * count * shard_rows * cols * half_width,
            bytes_accessed=4 * units * half_width * (count * shard_rows + cols),
            transcendentals=0,
        ),
        compiler_params=pltpu.CompilerParams(
            dimension_semantics=("arbitrary", "arbitrary"), vmem_limit_bytes=60 * 2**20
        ),
    )(plan, *operands)
    return given if raw else given[0]


def gathered(spectra, detector_valid, scale_coef):
    shard_rows = spectra.shape[1]
    half_width = spectra.shape[3] * spectra.shape[4]
    flattened = spectra.reshape(shard_rows, 2 * half_width)
    widened = flattened.astype(jnp.float32)
    power_mean = jnp.mean(widened * widened, axis=1) + 1e-06
    own_factor = detector_valid.reshape(shard_rows).astype(jnp.float32) * lax.rsqrt(power_mean)
    rows = lax.all_gather(flattened, "grp", axis=0, tiled=True)
    cols = lax.all_gather(flattened, "blk", axis=0, tiled=True)
    row_factor = lax.all_gather(own_factor, "grp", axis=0, tiled=True) * scale_coef
    col_factor = lax.all_gather(own_factor, "blk", axis=0, tiled=True)
    rotated = jnp.concatenate([-cols[:, half_width:], cols[:, :half_width]], axis=1)
    scaling = row_factor[:, None] * col_factor[None, :]
    parts = [
        lax.dot_general(rows, right, NT, preferred_element_type=jnp.float32) * scaling
        for right in (cols, rotated)
    ]
    return jnp.stack(parts)


def shards(spectra, detector_valid):
    shard_rows = spectra.shape[1]
    half_width = spectra.shape[3] * spectra.shape[4]
    blocks = lax.axis_size("blk")
    group_size = lax.axis_size("grp")
    scale_coef = 0.5 / math.sqrt(half_width)
    shape = (2, group_size, shard_rows, blocks * shard_rows)
    fits = shard_rows % 256 == 0 and half_width % 256 == 0 and group_size & (group_size - 1) == 0
    if blocks != 8 or not fits:
        return gathered(spectra, detector_valid, scale_coef).reshape(shape)

    devices = range(blocks)
    inner = [b for b in devices if 0 < b // 2 < blocks // 2 - 1]
    ends = [b for b in devices if b not in inner]
    me = lax.axis_index("blk")
    mine = lax.axis_index("grp")
    is_end = jnp.logical_or(me // 2 == 0, me // 2 == blocks // 2 - 1)

    def moved(value, axis, route):
        if isinstance(value, tuple):
            return tuple(moved(piece, axis, route) for piece in value)
        return lax.ppermute(value, axis, route)

    def swap(value, among, by):
        return moved(value, "blk", [(b, b ^ by) for b in among])

    def spread(value, by):
        return moved(value, "grp", [(g, g ^ by) for g in range(group_size)])

    def over_groups(value):
        arrays, by = {0: value}, group_size // 2
        while by:
            arrays.update({key ^ by: spread(array, by) for key, array in arrays.items()})
            by //= 2
        return [arrays[key] for key in range(group_size)]

    def either(inner_value, end_value):
        return jnp.where(is_end, end_value, inner_value)

    def put(out, columns, units):
        choice = [either(m, e) for m, e, _, _ in units]
        slots = [either(me ^ m, me ^ e) for _, _, m, e in units]
        return products(out, rows, columns, choice, slots, mine, blocks, scale_coef)

    (own,) = laid_out(spectra[0], detector_valid[0], 1)
    near = swap(own, devices, 2)
    beside = swap(own, devices, 1)
    across = swap(own, inner, 6)
    rows = over_groups(own)

    across_beside = swap(across, inner, 1)
    near_beside = swap(near, ends, 1)
    end_beside = swap(beside, ends, 2)
    far_inner = swap(across, inner, 2)
    far_end = swap(near, inner, 6)
    client = {0: near}
    if group_size > 1:
        client[group_size // 2] = spread(near, group_size // 2)

    out = put(
        None,
        [(own,), (near,), (beside,), (across,)],
        [(0, 0, 0, 0), (1, 1, 2, 2), (2, 2, 1, 1), (3, 0, 6, 5)],
    )
    half = shard_rows // 2
    far_end, end_beside, far_inner, client[group_size // 2], out = tied(
        far_end, end_beside, far_inner, client[group_size // 2], out
    )
    low = swap(far_end[:half], inner, 1)
    high = swap(end_beside[half:], inner, 6)
    far_inner_beside = swap(far_inner, ends, 1)
    by = group_size // 4
    while by:
        client.update({key ^ by: spread(array, by) for key, array in client.items()})
        by //= 2
    client = [client[key] for key in range(group_size)]
    out = put(
        out,
        [(across_beside,), (near_beside,), (end_beside,), (far_inner,)],
        [(0, 1, 7, 3), (2, 3, 3, 4)],
    )

    def serve(columns):
        return products(
            None, client, [columns], [me * 0], [me * 0], mine, blocks, scale_coef, raw=True
        )

    def deliver(block, unit_size):
        return swap(block.astype(jnp.float16), inner, 2), swap(unit_size, inner, 2)

    def place(out, sent, end_slot):
        block, unit_size = sent
        block = block.astype(jnp.float32) * unit_size[None, :, :1, :1]
        start = either(me ^ 5, me ^ end_slot) * shard_rows
        zero = jnp.zeros_like(start)
        return lax.dynamic_update_slice(out, block, (zero, zero, zero, start))

    far_end, out = tied(far_end, out)
    first = serve((far_end,))
    sent_a = deliver(*first)
    low, high, _ = tied(low, high, first[1])
    second = serve((low, high))
    sent_b = deliver(*second)
    out, _ = tied(out, second[1])
    out = put(out, [(far_end,)], [(0, 0, 4, 6)])
    out = place(out, sent_a, 6)
    out = place(out, sent_b, 7)
    out = put(out, [(low, high), (far_inner_beside,)], [(0, 1, 5, 5)])
    return out.reshape(shape)


def solution(mesh):
    return jax.shard_map(
        shards,
        mesh=mesh,
        in_specs=(P("grp", "blk", None, None, None), P("grp", "blk")),
        out_specs=P(None, None, "blk", "grp"),
        check_vma=False,
    )
```

```python
import functools
import math

import jax
import jax.numpy as jnp
from jax import lax
from jax.experimental import pallas as pl
from jax.experimental.pallas import tpu as pltpu
from jax.sharding import PartitionSpec as P


NT = (((1,), (1,)), ((), ()))
LANES = 128
FLOOR = 1e-30


def tile_of(size, most):
    tile = 1
    while tile * 2 <= most and size % (tile * 2) == 0:
        tile *= 2
    return tile


def tied(*values):
    return lax.optimization_barrier(values)


def split_in_three(value):
    parts = []
    for _ in range(2):
        part = value.astype(jnp.bfloat16).astype(jnp.float32)
        parts.append(part)
        value = value - part
    return parts + [value]


def laid_out_body(per_piece, spectra_ref, flags_ref, whole_ref, *piece_refs):
    high, parts, bins, taps = spectra_ref.shape
    half_width = bins * taps

    def fill(out_ref):
        power = jnp.zeros((high, 1), jnp.float32)
        for part in range(parts):
            flat = spectra_ref[:, part].reshape(high, half_width)
            out_ref[:, part * half_width : (part + 1) * half_width] = flat
            widened = flat.astype(jnp.float32)
            power = power + jnp.sum(widened * widened, axis=1, keepdims=True)
        power_mean = power / (parts * half_width)
        factor = flags_ref[...].astype(jnp.float32) * lax.rsqrt(power_mean + 1e-06)
        norm = lax.rsqrt(jnp.maximum(power_mean, FLOOR))
        lane = lax.broadcasted_iota(jnp.int32, (high, LANES), 1)
        marks = jnp.zeros((high, LANES), jnp.float32)
        for index, value in enumerate(split_in_three(factor) + split_in_three(norm)):
            marks = jnp.where(lane == index, value, marks)
        out_ref[:, parts * half_width :] = marks.astype(jnp.bfloat16)

    fill(whole_ref)
    for piece, out_ref in enumerate(piece_refs):

        @pl.when(pl.program_id(0) // per_piece == piece)
        def _():
            out_ref[...] = whole_ref[...]


def laid_out(spectra, flags, pieces):
    rows, parts, bins, taps = spectra.shape
    width = parts * bins * taps + LANES
    high = tile_of(rows // pieces, 64)
    per_piece = rows // pieces // high

    def place(piece):
        first = piece * per_piece
        return lambda i: (jnp.clip(i - first, 0, per_piece - 1), 0)

    return pl.pallas_call(
        functools.partial(laid_out_body, per_piece),
        grid=(rows // high,),
        in_specs=[
            pl.BlockSpec((high, parts, bins, taps), lambda i: (i, 0, 0, 0)),
            pl.BlockSpec((high, 1), lambda i: (i, 0)),
        ],
        out_specs=[pl.BlockSpec((high, width), lambda i: (i, 0))]
        + [pl.BlockSpec((high, width), place(piece)) for piece in range(pieces)],
        out_shape=[jax.ShapeDtypeStruct((rows, width), spectra.dtype)]
        + [jax.ShapeDtypeStruct((rows // pieces, width), spectra.dtype)] * pieces,
    )(spectra, flags.reshape(rows, 1))


def products_body(sizes, scale_coef, raw, plan_ref, *refs):
    shapes, at_once, known, units = sizes
    refs = list(refs)
    rows, at = [], 0
    for shape in shapes:
        rows.append(refs[at : at + len(shape)])
        at += len(shape)
    columns = refs[at : at + known]
    held, right, col_marks, staged, row_sems, col_sems, out_sems = refs[-7:]
    outs = refs[-9:-7] if raw else refs[-8:-7]
    unit, part = pl.program_id(0), pl.program_id(1)
    parts = len(rows) // at_once
    now = unit * parts + part
    shard_rows = held.shape[1] // at_once
    cols, half_width = right.shape[1] // 2, right.shape[2] // 2
    half_cols = cols // 2

    def row_copies(index, row, slot):
        copies, top = [], row * shard_rows
        for number, piece in enumerate(rows[index]):
            where = held.at[slot, pl.ds(top, piece.shape[0])]
            copies.append(pltpu.make_async_copy(piece, where, row_sems.at[slot, row, number]))
            top += piece.shape[0]
        return copies

    def start_rows(which, slot):
        for index in range(parts):

            @pl.when(which == index)
            def _():
                for row in range(at_once):
                    for copy in row_copies(index * at_once + row, row, slot):
                        copy.start()

    def col_copies(source, half, slot):
        top = half * half_cols
        real = source.at[:, pl.ds(0, half_width)]
        imag = source.at[:, pl.ds(half_width, half_width)]
        marks = source.at[:, pl.ds(2 * half_width, LANES)]
        places = [
            (real, right.at[slot, pl.ds(top, half_cols), pl.ds(0, half_width)]),
            (imag, right.at[slot, pl.ds(top, half_cols), pl.ds(half_width, half_width)]),
            (real, right.at[slot, pl.ds(cols + top, half_cols), pl.ds(half_width, half_width)]),
            (marks, col_marks.at[slot, pl.ds(top, half_cols)]),
        ]
        return [
            pltpu.make_async_copy(start, end, col_sems.at[slot, half, kind])
            for kind, (start, end) in enumerate(places)
        ]

    def start_cols(which, slot):
        for half in range(2):
            for index in range(known):

                @pl.when(plan_ref[2 * which + half] == index)
                def _():
                    for copy in col_copies(columns[index], half, slot):
                        copy.start()

    def out_copies(slot):
        copies = []
        for row in range(at_once):
            group = plan_ref[4 * units + part * at_once + row]
            for half in range(2):
                start = plan_ref[2 * units + 2 * unit + half] * half_cols
                lanes = pl.ds(pl.multiple_of(start, half_cols), half_cols)
                source = staged.at[slot, :, row, :, pl.ds(half * half_cols, half_cols)]
                target = outs[0].at[:, group, :, lanes]
                copies.append(pltpu.make_async_copy(source, target, out_sems.at[slot, row, half]))
        return copies

    slot, col_slot = lax.rem(now, 2), lax.rem(unit, 2)

    @pl.when(now == 0)
    def _():
        start_rows(0, 0)
        start_cols(0, 0)

    @pl.when(now + 1 < units * parts)
    def _():
        start_rows(lax.rem(part + 1, parts), lax.rem(now + 1, 2))

    @pl.when(jnp.logical_and(part == 0, unit + 1 < units))
    def _():
        start_cols(unit + 1, lax.rem(unit + 1, 2))

    @pl.when(part == 0)
    def _():
        for half in range(2):
            for copy in col_copies(columns[0], half, col_slot):
                copy.wait()
        right[col_slot, cols:, :half_width] = -right[col_slot, :cols, half_width:]

    for row in range(at_once):
        for copy in row_copies(row, row, slot):
            copy.wait()

    left = held[slot, :, : 2 * half_width]
    product = lax.dot_general(left, right[col_slot], NT, preferred_element_type=jnp.float32)

    @pl.when(now >= 2)
    def _():
        for copy in out_copies(slot):
            copy.wait()

    def sums(values, axis):
        def one(first):
            take = [lax.slice_in_dim(values, i, i + 1, axis=axis) for i in range(first, first + 3)]
            return (take[2] + take[1]) + take[0]

        return one(0), one(3)

    col_factor, col_norm = sums(col_marks[col_slot].astype(jnp.float32).T, 0)
    for row in range(at_once):
        top = row * shard_rows
        marks = held[slot, pl.ds(top, shard_rows), pl.ds(2 * half_width, LANES)]
        row_factor, row_norm = sums(marks.astype(jnp.float32), 1)
        scaling = (row_factor * scale_coef) * col_factor
        if raw:
            bound = jnp.max(row_factor / row_norm, axis=0, keepdims=True)
            bound = bound * jnp.max(col_factor / col_norm, axis=1, keepdims=True)
            unit_size = jnp.maximum(bound * (2 * half_width * scale_coef), FLOOR) / 32768
            outs[1][row] = jnp.broadcast_to(unit_size, outs[1].shape[1:])
            scaling = scaling * (1 / unit_size)
        staged[slot, 0, row] = product[top : top + shard_rows, :cols] * scaling
        staged[slot, 1, row] = product[top : top + shard_rows, cols:] * scaling

    for copy in out_copies(slot):
        copy.start()

    @pl.when(now == units * parts - 1)
    def _():
        for copy in out_copies(lax.rem(now + 1, 2)) + out_copies(slot):
            copy.wait()


def products(out, rows, columns, choice, slots, mine, blocks, scale_coef, raw=False):
    shard_rows = sum(piece.shape[0] for piece in rows[0])
    width = rows[0][0].shape[1]
    half_width = (width - LANES) // 2
    units, count = len(choice) // 2, len(rows)
    at_once = 2 if units > 1 and count > 1 else 1
    parts = count // at_once
    cols = 2 * columns[0].shape[0]
    whole = pl.BlockSpec(memory_space=pl.ANY)
    operands = [piece for pieces in rows for piece in pieces] + list(columns)
    aliases = {}
    if out is not None:
        aliases = {1 + len(operands): 0}
        operands.append(out)
    groups = [mine ^ j for j in range(count)]
    plan = jnp.stack(list(choice) + list(slots) + groups).astype(jnp.int32)
    shape = (2, count, shard_rows, cols if raw else shard_rows * blocks)
    out_shape = [jax.ShapeDtypeStruct(shape, jnp.float32)]
    out_specs = [whole]
    if raw:
        out_shape.append(jax.ShapeDtypeStruct((count, 8, LANES), jnp.float32))
        out_specs.append(
            pl.BlockSpec((at_once, 8, LANES), lambda i, j, s: (s[4 * units + j], 0, 0))
        )
    shapes = [[piece.shape[0] for piece in pieces] for pieces in rows]
    most = max(len(pieces) for pieces in rows)
    given = pl.pallas_call(
        functools.partial(products_body, (shapes, at_once, len(columns), units), scale_coef, raw),
        grid_spec=pltpu.PrefetchScalarGridSpec(
            num_scalar_prefetch=1,
            grid=(units, parts),
            in_specs=[whole] * len(operands),
            out_specs=out_specs,
            scratch_shapes=[
                pltpu.VMEM((2, at_once * shard_rows, width), rows[0][0].dtype),
                pltpu.VMEM((2, 2 * cols, 2 * half_width), rows[0][0].dtype),
                pltpu.VMEM((2, cols, LANES), rows[0][0].dtype),
                pltpu.VMEM((2, 2, at_once, shard_rows, cols), jnp.float32),
                pltpu.SemaphoreType.DMA((2, at_once, most)),
                pltpu.SemaphoreType.DMA((2, 2, 4)),
                pltpu.SemaphoreType.DMA((2, at_once, 2)),
            ],
        ),
        out_shape=out_shape,
        input_output_aliases=aliases,
        cost_estimate=pl.CostEstimate(
            flops=8 * units * count * shard_rows * cols * half_width,
            bytes_accessed=4 * units * half_width * (count * shard_rows + cols),
            transcendentals=0,
        ),
        compiler_params=pltpu.CompilerParams(
            dimension_semantics=("arbitrary", "arbitrary"), vmem_limit_bytes=60 * 2**20
        ),
    )(plan, *operands)
    return given if raw else given[0]


def gathered(spectra, detector_valid, scale_coef):
    shard_rows = spectra.shape[1]
    half_width = spectra.shape[3] * spectra.shape[4]
    flattened = spectra.reshape(shard_rows, 2 * half_width)
    widened = flattened.astype(jnp.float32)
    power_mean = jnp.mean(widened * widened, axis=1) + 1e-06
    own_factor = detector_valid.reshape(shard_rows).astype(jnp.float32) * lax.rsqrt(power_mean)
    rows = lax.all_gather(flattened, "grp", axis=0, tiled=True)
    cols = lax.all_gather(flattened, "blk", axis=0, tiled=True)
    row_factor = lax.all_gather(own_factor, "grp", axis=0, tiled=True) * scale_coef
    col_factor = lax.all_gather(own_factor, "blk", axis=0, tiled=True)
    rotated = jnp.concatenate([-cols[:, half_width:], cols[:, :half_width]], axis=1)
    scaling = row_factor[:, None] * col_factor[None, :]
    parts = [
        lax.dot_general(rows, right, NT, preferred_element_type=jnp.float32) * scaling
        for right in (cols, rotated)
    ]
    return jnp.stack(parts)


def shards(spectra, detector_valid):
    shard_rows = spectra.shape[1]
    half_width = spectra.shape[3] * spectra.shape[4]
    blocks = lax.axis_size("blk")
    group_size = lax.axis_size("grp")
    scale_coef = 0.5 / math.sqrt(half_width)
    shape = (2, group_size, shard_rows, blocks * shard_rows)
    fits = shard_rows % 256 == 0 and half_width % 128 == 0 and group_size & (group_size - 1) == 0
    if blocks != 8 or group_size < 2 or not fits:
        return gathered(spectra, detector_valid, scale_coef).reshape(shape)

    devices = range(blocks)
    inner = [b for b in devices if 0 < b // 2 < blocks // 2 - 1]
    ends = [b for b in devices if b not in inner]
    me = lax.axis_index("blk")
    mine = lax.axis_index("grp")
    is_end = jnp.logical_or(me // 2 == 0, me // 2 == blocks // 2 - 1)

    def moved(value, axis, route):
        if isinstance(value, tuple):
            return tuple(moved(piece, axis, route) for piece in value)
        return lax.ppermute(value, axis, route)

    def swap(value, among, by):
        return moved(value, "blk", [(b, b ^ by) for b in among])

    def spread(value, by):
        return moved(value, "grp", [(g, g ^ by) for g in range(group_size)])

    def begun(value):
        return {0: value, group_size // 2: spread(value, group_size // 2)}

    def finished(arrays):
        by = group_size // 4
        while by:
            arrays = arrays | {key ^ by: spread(array, by) for key, array in arrays.items()}
            by //= 2
        return [arrays[key] for key in range(group_size)]

    def held_for(value, *after):
        return tied(value, *after)[0]

    def either(inner_value, end_value):
        return jnp.where(is_end, end_value, inner_value)

    def put(out, columns, units):
        halves = [half for column in columns for half in column]
        choice, slots = [], []
        for inner_half, end_half in units:
            choice.append(either(*(2 * c + h for c, h, _ in (inner_half, end_half))))
            slots.append(
                either(*(2 * (me ^ slot) + h for _, h, slot in (inner_half, end_half)))
            )
        return products(out, rows, halves, choice, slots, mine, blocks, scale_coef)

    def both(inner_column, inner_slot, end_column, end_slot):
        return [((inner_column, h, inner_slot), (end_column, h, end_slot)) for h in (0, 1)]

    whole, *own = laid_out(spectra[0], detector_valid[0], 2)
    own = tuple(own)
    near = swap(own, devices, 2)
    beside = swap(own, devices, 1)
    across = swap(own, inner, 6)
    rows = begun(whole)
    last = group_size // 2
    rows[last] = held_for(rows[last], *near, *beside, *across)
    rows = [(array,) for array in finished(rows)]

    far_end = swap(near, inner, 6)
    end_beside = swap(beside, ends, 2)
    far_inner = swap(across, inner, 2)
    across_beside = swap(across, inner, 1)
    near_beside = swap(near, ends, 1)
    client = begun(near)

    out = put(
        None,
        [own, near, beside, across],
        both(0, 0, 0, 0) + both(1, 2, 1, 2) + both(2, 1, 2, 1) + both(3, 6, 0, 5),
    )
    out = put(
        out,
        [far_end[:1] * 2, end_beside[:1] * 2, far_inner[:1] * 2, near_beside[:1] * 2],
        [((0, 0, 4), (2, 0, 4)), ((1, 0, 3), (3, 0, 3))],
    )
    *held, out = tied(
        far_end[0], end_beside[1], far_inner[0], across_beside[1], *client[last], out
    )
    client[last] = tuple(held[4:])
    low = swap(held[0], inner, 1)
    high = swap(held[1], inner, 6)
    low_beside = swap(held[2], ends, 1)
    high_beside = swap(held[3], inner, 2)
    client = finished(client)

    def serve(columns):
        zero = me * 0
        pick = [zero, zero + 1]
        return products(None, client, columns, pick, pick, mine, blocks, scale_coef, raw=True)

    def deliver(block, unit_size):
        return swap(block.astype(jnp.float16), inner, 2), swap(unit_size, inner, 2)

    def place(out, sent, end_slot):
        block, unit_size = sent
        block = block.astype(jnp.float32) * unit_size[None, :, :1, :1]
        start = (me ^ end_slot) * shard_rows
        starts = [jnp.zeros_like(start)] * 3 + [start]
        kept = lax.dynamic_slice(out, starts, block.shape)
        return lax.dynamic_update_slice(out, jnp.where(is_end, block, kept), starts)

    first = serve(far_end)
    sent_a = deliver(*first)
    out, _ = tied(out, first[1])
    out = put(
        out,
        [across_beside, far_end, end_beside, far_inner, near_beside],
        both(0, 7, 3, 6) + [((1, 1, 4), (3, 1, 4)), ((2, 1, 3), (4, 1, 3))],
    )
    low, high, low_beside, high_beside, out = tied(low, high, low_beside, high_beside, out)
    second = serve((low, high))
    sent_b = deliver(*second)
    out, _ = tied(out, second[1])
    out = put(out, [(low, high), (low_beside, high_beside)], both(0, 5, 1, 5))
    out = place(out, sent_a, 6)
    out = place(out, sent_b, 7)
    return out.reshape(shape)


def solution(mesh):
    return jax.shard_map(
        shards,
        mesh=mesh,
        in_specs=(P("grp", "blk", None, None, None), P("grp", "blk")),
        out_specs=P(None, None, "blk", "grp"),
        check_vma=False,
    )
```

```python
import functools
import math

import jax
import jax.numpy as jnp
from jax import lax
from jax.experimental import pallas as pl
from jax.experimental.pallas import tpu as pltpu
from jax.sharding import PartitionSpec as P


NT = (((1,), (1,)), ((), ()))
LANES = 128
FLOOR = 1e-30


def tile_of(size, most):
    tile = 1
    while tile * 2 <= most and size % (tile * 2) == 0:
        tile *= 2
    return tile


def passed_body(value_ref, out_ref):
    out_ref[...] = value_ref[...]


def passed(number):
    block = jnp.broadcast_to(number, (8, LANES)).astype(jnp.int32)
    out = pl.pallas_call(passed_body, out_shape=jax.ShapeDtypeStruct(block.shape, jnp.int32))(block)
    return out[0, 0]


def tied(*values):
    return lax.optimization_barrier(values)


def split_in_three(value):
    parts = []
    for _ in range(2):
        part = value.astype(jnp.bfloat16).astype(jnp.float32)
        parts.append(part)
        value = value - part
    return parts + [value]


def laid_out_body(per_piece, spectra_ref, flags_ref, whole_ref, *piece_refs):
    high, parts, bins, taps = spectra_ref.shape
    half_width = bins * taps

    def fill(out_ref):
        power = jnp.zeros((high, 1), jnp.float32)
        for part in range(parts):
            flat = spectra_ref[:, part].reshape(high, half_width)
            out_ref[:, part * half_width : (part + 1) * half_width] = flat
            widened = flat.astype(jnp.float32)
            power = power + jnp.sum(widened * widened, axis=1, keepdims=True)
        power_mean = power / (parts * half_width)
        factor = flags_ref[...].astype(jnp.float32) * lax.rsqrt(power_mean + 1e-06)
        norm = lax.rsqrt(jnp.maximum(power_mean, FLOOR))
        lane = lax.broadcasted_iota(jnp.int32, (high, LANES), 1)
        marks = jnp.zeros((high, LANES), jnp.float32)
        for index, value in enumerate(split_in_three(factor) + split_in_three(norm)):
            marks = jnp.where(lane == index, value, marks)
        out_ref[:, parts * half_width :] = marks.astype(jnp.bfloat16)

    fill(whole_ref)
    for piece, out_ref in enumerate(piece_refs):

        @pl.when(pl.program_id(0) // per_piece == piece)
        def _():
            out_ref[...] = whole_ref[...]


def laid_out(spectra, flags, pieces):
    rows, parts, bins, taps = spectra.shape
    width = parts * bins * taps + LANES
    high = tile_of(rows // pieces, 64)
    per_piece = rows // pieces // high

    def place(piece):
        first = piece * per_piece
        return lambda i: (jnp.clip(i - first, 0, per_piece - 1), 0)

    return pl.pallas_call(
        functools.partial(laid_out_body, per_piece),
        grid=(rows // high,),
        in_specs=[
            pl.BlockSpec((high, parts, bins, taps), lambda i: (i, 0, 0, 0)),
            pl.BlockSpec((high, 1), lambda i: (i, 0)),
        ],
        out_specs=[pl.BlockSpec((high, width), lambda i: (i, 0))]
        + [pl.BlockSpec((high, width), place(piece)) for piece in range(pieces)],
        out_shape=[jax.ShapeDtypeStruct((rows, width), spectra.dtype)]
        + [jax.ShapeDtypeStruct((rows // pieces, width), spectra.dtype)] * pieces,
    )(spectra, flags.reshape(rows, 1))


def products_body(sizes, scale_coef, raw, plan_ref, *refs):
    shapes, at_once, known, units = sizes
    refs = list(refs)
    rows, at = [], 0
    for shape in shapes:
        rows.append(refs[at : at + len(shape)])
        at += len(shape)
    columns = refs[at : at + known]
    held, right, col_marks, staged, row_sems, col_sems, out_sems = refs[-7:]
    outs = refs[-9:-7] if raw else refs[-8:-7]
    unit, part = pl.program_id(0), pl.program_id(1)
    parts = len(rows) // at_once
    now = unit * parts + part
    shard_rows = held.shape[1] // at_once
    cols, half_width = right.shape[1] // 2, right.shape[2] // 2
    half_cols = cols // 2

    def row_copies(index, row, slot):
        copies, top = [], row * shard_rows
        for number, piece in enumerate(rows[index]):
            where = held.at[slot, pl.ds(top, piece.shape[0])]
            copies.append(pltpu.make_async_copy(piece, where, row_sems.at[slot, row, number]))
            top += piece.shape[0]
        return copies

    def start_rows(which, slot):
        for index in range(parts):

            @pl.when(which == index)
            def _():
                for row in range(at_once):
                    for copy in row_copies(index * at_once + row, row, slot):
                        copy.start()

    def col_copies(source, half, slot):
        top = half * half_cols
        real = source.at[:, pl.ds(0, half_width)]
        imag = source.at[:, pl.ds(half_width, half_width)]
        marks = source.at[:, pl.ds(2 * half_width, LANES)]
        places = [
            (real, right.at[slot, pl.ds(top, half_cols), pl.ds(0, half_width)]),
            (imag, right.at[slot, pl.ds(top, half_cols), pl.ds(half_width, half_width)]),
            (real, right.at[slot, pl.ds(cols + top, half_cols), pl.ds(half_width, half_width)]),
            (marks, col_marks.at[slot, pl.ds(top, half_cols)]),
        ]
        return [
            pltpu.make_async_copy(start, end, col_sems.at[slot, half, kind])
            for kind, (start, end) in enumerate(places)
        ]

    def start_cols(which, slot):
        for half in range(2):
            for index in range(known):

                @pl.when(plan_ref[2 * which + half] == index)
                def _():
                    for copy in col_copies(columns[index], half, slot):
                        copy.start()

    def out_copies(slot):
        copies = []
        for row in range(at_once):
            group = plan_ref[4 * units + part * at_once + row]
            for half in range(2):
                start = plan_ref[2 * units + 2 * unit + half] * half_cols
                lanes = pl.ds(pl.multiple_of(start, half_cols), half_cols)
                source = staged.at[slot, :, row, :, pl.ds(half * half_cols, half_cols)]
                target = outs[0].at[:, group, :, lanes]
                copies.append(pltpu.make_async_copy(source, target, out_sems.at[slot, row, half]))
        return copies

    slot, col_slot = lax.rem(now, 2), lax.rem(unit, 2)

    @pl.when(now == 0)
    def _():
        start_rows(0, 0)
        start_cols(0, 0)

    @pl.when(now + 1 < units * parts)
    def _():
        start_rows(lax.rem(part + 1, parts), lax.rem(now + 1, 2))

    @pl.when(jnp.logical_and(part == 0, unit + 1 < units))
    def _():
        start_cols(unit + 1, lax.rem(unit + 1, 2))

    @pl.when(part == 0)
    def _():
        for half in range(2):
            for copy in col_copies(columns[0], half, col_slot):
                copy.wait()
        right[col_slot, cols:, :half_width] = -right[col_slot, :cols, half_width:]

    for row in range(at_once):
        for copy in row_copies(row, row, slot):
            copy.wait()

    left = held[slot, :, : 2 * half_width]
    product = lax.dot_general(left, right[col_slot], NT, preferred_element_type=jnp.float32)

    @pl.when(now >= 2)
    def _():
        for copy in out_copies(slot):
            copy.wait()

    def sums(values, axis):
        def one(first):
            take = [lax.slice_in_dim(values, i, i + 1, axis=axis) for i in range(first, first + 3)]
            return (take[2] + take[1]) + take[0]

        return one(0), one(3)

    col_factor, col_norm = sums(col_marks[col_slot].astype(jnp.float32).T, 0)
    for row in range(at_once):
        top = row * shard_rows
        marks = held[slot, pl.ds(top, shard_rows), pl.ds(2 * half_width, LANES)]
        row_factor, row_norm = sums(marks.astype(jnp.float32), 1)
        scaling = (row_factor * scale_coef) * col_factor
        if raw:
            bound = jnp.max(row_factor / row_norm, axis=0, keepdims=True)
            bound = bound * jnp.max(col_factor / col_norm, axis=1, keepdims=True)
            unit_size = jnp.maximum(bound * (2 * half_width * scale_coef), FLOOR) / 32768
            group = plan_ref[4 * units + part * at_once + row]
            outs[1][group] = jnp.broadcast_to(unit_size, outs[1].shape[1:])
            scaling = scaling * (1 / unit_size)
        staged[slot, 0, row] = product[top : top + shard_rows, :cols] * scaling
        staged[slot, 1, row] = product[top : top + shard_rows, cols:] * scaling

    for copy in out_copies(slot):
        copy.start()

    @pl.when(now == units * parts - 1)
    def _():
        for copy in out_copies(lax.rem(now + 1, 2)) + out_copies(slot):
            copy.wait()


def products(out, rows, columns, choice, slots, mine, blocks, scale_coef, raw=False):
    shard_rows = sum(piece.shape[0] for piece in rows[0])
    width = rows[0][0].shape[1]
    half_width = (width - LANES) // 2
    units, count = len(choice) // 2, len(rows)
    at_once = 2 if units > 1 and count > 1 else 1
    parts = count // at_once
    cols = 2 * columns[0].shape[0]
    whole = pl.BlockSpec(memory_space=pl.ANY)
    operands = [piece for pieces in rows for piece in pieces] + list(columns)
    aliases = {}
    if out is not None:
        aliases = {1 + len(operands): 0}
        operands.append(out)
    groups = [mine ^ j for j in range(count)]
    plan = jnp.stack(list(choice) + list(slots) + groups).astype(jnp.int32)
    shape = (2, count, shard_rows, cols if raw else shard_rows * blocks)
    out_shape = [jax.ShapeDtypeStruct(shape, jnp.float32)]
    out_specs = [whole]
    if raw:
        out_shape.append(jax.ShapeDtypeStruct((count, 8, LANES), jnp.float32))
        out_specs.append(
            pl.BlockSpec((count, 8, LANES), lambda i, j, s: (0, 0, 0))
        )
    shapes = [[piece.shape[0] for piece in pieces] for pieces in rows]
    most = max(len(pieces) for pieces in rows)
    given = pl.pallas_call(
        functools.partial(products_body, (shapes, at_once, len(columns), units), scale_coef, raw),
        grid_spec=pltpu.PrefetchScalarGridSpec(
            num_scalar_prefetch=1,
            grid=(units, parts),
            in_specs=[whole] * len(operands),
            out_specs=out_specs,
            scratch_shapes=[
                pltpu.VMEM((2, at_once * shard_rows, width), rows[0][0].dtype),
                pltpu.VMEM((2, 2 * cols, 2 * half_width), rows[0][0].dtype),
                pltpu.VMEM((2, cols, LANES), rows[0][0].dtype),
                pltpu.VMEM((2, 2, at_once, shard_rows, cols), jnp.float32),
                pltpu.SemaphoreType.DMA((2, at_once, most)),
                pltpu.SemaphoreType.DMA((2, 2, 4)),
                pltpu.SemaphoreType.DMA((2, at_once, 2)),
            ],
        ),
        out_shape=out_shape,
        input_output_aliases=aliases,
        cost_estimate=pl.CostEstimate(
            flops=8 * units * count * shard_rows * cols * half_width,
            bytes_accessed=4 * units * half_width * (count * shard_rows + cols),
            transcendentals=0,
        ),
        compiler_params=pltpu.CompilerParams(
            dimension_semantics=("arbitrary", "arbitrary"), vmem_limit_bytes=60 * 2**20
        ),
    )(plan, *operands)
    return given if raw else given[0]


def gathered(spectra, detector_valid, scale_coef):
    shard_rows = spectra.shape[1]
    half_width = spectra.shape[3] * spectra.shape[4]
    flattened = spectra.reshape(shard_rows, 2 * half_width)
    widened = flattened.astype(jnp.float32)
    power_mean = jnp.mean(widened * widened, axis=1) + 1e-06
    own_factor = detector_valid.reshape(shard_rows).astype(jnp.float32) * lax.rsqrt(power_mean)
    rows = lax.all_gather(flattened, "grp", axis=0, tiled=True)
    cols = lax.all_gather(flattened, "blk", axis=0, tiled=True)
    row_factor = lax.all_gather(own_factor, "grp", axis=0, tiled=True) * scale_coef
    col_factor = lax.all_gather(own_factor, "blk", axis=0, tiled=True)
    rotated = jnp.concatenate([-cols[:, half_width:], cols[:, :half_width]], axis=1)
    scaling = row_factor[:, None] * col_factor[None, :]
    parts = [
        lax.dot_general(rows, right, NT, preferred_element_type=jnp.float32) * scaling
        for right in (cols, rotated)
    ]
    return jnp.stack(parts)


def shards(spectra, detector_valid):
    shard_rows = spectra.shape[1]
    half_width = spectra.shape[3] * spectra.shape[4]
    blocks = lax.axis_size("blk")
    group_size = lax.axis_size("grp")
    scale_coef = 0.5 / math.sqrt(half_width)
    shape = (2, group_size, shard_rows, blocks * shard_rows)
    fits = shard_rows % 256 == 0 and half_width % 128 == 0 and group_size & (group_size - 1) == 0
    if blocks != 8 or group_size < 2 or not fits:
        return gathered(spectra, detector_valid, scale_coef).reshape(shape)

    devices = range(blocks)
    inner = [b for b in devices if 0 < b // 2 < blocks // 2 - 1]
    ends = [b for b in devices if b not in inner]
    me = lax.axis_index("blk")
    mine = lax.axis_index("grp")
    is_end = jnp.logical_or(me // 2 == 0, me // 2 == blocks // 2 - 1)

    def moved(value, axis, route):
        if not isinstance(value, tuple):
            return lax.ppermute(value, axis, route)
        pieces = []
        for piece in value:
            pieces.append(lax.ppermute(piece, axis, route))
        return tuple(pieces)

    def swap(value, among, by):
        return moved(value, "blk", [(b, b ^ by) for b in among])

    def spread(value, by):
        return moved(value, "grp", [(g, g ^ by) for g in range(group_size)])

    def begun(value):
        return {0: value, group_size // 2: spread(value, group_size // 2)}

    def finished(arrays):
        by = group_size // 4
        while by:
            arrays = arrays | {key ^ by: spread(array, by) for key, array in arrays.items()}
            by //= 2
        return [arrays[key] for key in range(group_size)]

    def held_for(value, *after):
        return tied(value, *after)[0]

    def either(inner_value, end_value):
        return jnp.where(is_end, end_value, inner_value)

    def put(out, columns, units, me=me):
        halves = [half for column in columns for half in column]
        choice, slots = [], []
        for inner_half, end_half in units:
            choice.append(either(*(2 * c + h for c, h, _ in (inner_half, end_half))))
            slots.append(
                either(*(2 * (me ^ slot) + h for _, h, slot in (inner_half, end_half)))
            )
        return products(out, rows, halves, choice, slots, mine, blocks, scale_coef)

    def both(inner_column, inner_slot, end_column, end_slot):
        return [((inner_column, h, inner_slot), (end_column, h, end_slot)) for h in (0, 1)]

    whole, *own = laid_out(spectra[0], detector_valid[0], 2)
    own = tuple(own)
    near = swap(own, devices, 2)
    beside = swap(own, devices, 1)
    across = swap(own, inner, 6)
    rows = begun(whole)
    last = group_size // 2
    rows[last] = held_for(rows[last], *near, *beside, *across)
    rows = [(array,) for array in finished(rows)]

    far_end = swap(near, inner, 6)
    end_beside = swap(beside, ends, 2)
    far_inner = swap(across, inner, 2)
    across_beside = swap(across, inner, 1)
    near_beside = swap(near, ends, 1)
    client = begun(near)

    marked = passed(me)
    out = put(
        None,
        [own, near, beside, across],
        both(0, 0, 0, 0) + both(1, 2, 1, 2) + both(2, 1, 2, 1) + both(3, 6, 0, 5),
        marked,
    )
    *held, first_out = tied(far_end[0], far_inner[0], client[last][0], out)
    low = swap(held[0], inner, 1)
    low_beside = swap(held[1], ends, 1)
    firsts = finished({0: near[0], last: held[2]})
    out = put(
        first_out,
        [far_end[:1] * 2, end_beside[:1] * 2, far_inner[:1] * 2, near_beside[:1] * 2],
        [((0, 0, 4), (2, 0, 4)), ((1, 0, 3), (3, 0, 3))],
    )
    *held, out = tied(end_beside[1], across_beside[1], client[last][1], out)
    high = swap(held[0], inner, 6)
    high_beside = swap(held[1], inner, 2)
    seconds = finished({0: near[1], last: held[2]})
    client = list(zip(firsts, seconds))

    def serve(columns):
        zero = me * 0
        pick = [zero, zero + 1]
        return products(None, client, columns, pick, pick, mine, blocks, scale_coef, raw=True)

    def deliver(block, unit_size):
        return swap(block.astype(jnp.float16), inner, 2), swap(unit_size, inner, 2)

    def place(out, sent, end_slot):
        block, unit_size = sent
        block = block.astype(jnp.float32) * unit_size[None, :, :1, :1]
        start = (me ^ end_slot) * shard_rows
        starts = [jnp.zeros_like(start)] * 3 + [start]
        kept = lax.dynamic_slice(out, starts, block.shape)
        return lax.dynamic_update_slice(out, jnp.where(is_end, block, kept), starts)

    first = serve(far_end)
    sent_a = deliver(*first)
    out, _ = tied(out, first[1])
    out = put(
        out,
        [across_beside, far_end, end_beside, far_inner, near_beside],
        both(0, 7, 3, 6) + [((1, 1, 4), (3, 1, 4)), ((2, 1, 3), (4, 1, 3))],
    )
    low, high, low_beside, high_beside, out = tied(low, high, low_beside, high_beside, out)
    second = serve((low, high))
    sent_b = deliver(*second)
    out, _ = tied(out, second[1])
    out = put(out, [(low, high), (low_beside, high_beside)], both(0, 5, 1, 5))
    out = place(out, sent_a, 6)
    out = place(out, sent_b, 7)
    return out.reshape(shape)


def solution(mesh):
    return jax.shard_map(
        shards,
        mesh=mesh,
        in_specs=(P("grp", "blk", None, None, None), P("grp", "blk")),
        out_specs=P(None, None, "blk", "grp"),
        check_vma=False,
    )
```

```python
import functools
import math

import jax
import jax.numpy as jnp
from jax import lax
from jax.experimental import pallas as pl
from jax.experimental.pallas import tpu as pltpu
from jax.sharding import PartitionSpec as P


NT = (((1,), (1,)), ((), ()))
LANES = 128
FLOOR = 1e-30


def tile_of(size, most):
    tile = 1
    while tile * 2 <= most and size % (tile * 2) == 0:
        tile *= 2
    return tile


def passed_body(count, *refs):
    for value_ref, out_ref in zip(refs[:count], refs[count:]):
        out_ref[...] = value_ref[...]


def passed(values):
    return pl.pallas_call(
        functools.partial(passed_body, len(values)),
        out_shape=[jax.ShapeDtypeStruct(value.shape, value.dtype) for value in values],
    )(*values)


def tied(*values):
    return lax.optimization_barrier(values)


def split_in_three(value):
    parts = []
    for _ in range(2):
        part = value.astype(jnp.bfloat16).astype(jnp.float32)
        parts.append(part)
        value = value - part
    return parts + [value]


def laid_out_body(per_piece, spectra_ref, flags_ref, whole_ref, *piece_refs):
    high, parts, bins, taps = spectra_ref.shape
    half_width = bins * taps

    def fill(out_ref):
        power = jnp.zeros((high, 1), jnp.float32)
        for part in range(parts):
            flat = spectra_ref[:, part].reshape(high, half_width)
            out_ref[:, part * half_width : (part + 1) * half_width] = flat
            widened = flat.astype(jnp.float32)
            power = power + jnp.sum(widened * widened, axis=1, keepdims=True)
        power_mean = power / (parts * half_width)
        factor = flags_ref[...].astype(jnp.float32) * lax.rsqrt(power_mean + 1e-06)
        norm = lax.rsqrt(jnp.maximum(power_mean, FLOOR))
        lane = lax.broadcasted_iota(jnp.int32, (high, LANES), 1)
        marks = jnp.zeros((high, LANES), jnp.float32)
        for index, value in enumerate(split_in_three(factor) + split_in_three(norm)):
            marks = jnp.where(lane == index, value, marks)
        out_ref[:, parts * half_width :] = marks.astype(jnp.bfloat16)

    fill(whole_ref)
    for piece, out_ref in enumerate(piece_refs):

        @pl.when(pl.program_id(0) // per_piece == piece)
        def _():
            out_ref[...] = whole_ref[...]


def laid_out(spectra, flags, pieces):
    rows, parts, bins, taps = spectra.shape
    width = parts * bins * taps + LANES
    high = tile_of(rows // pieces, 64)
    per_piece = rows // pieces // high

    def place(piece):
        first = piece * per_piece
        return lambda i: (jnp.clip(i - first, 0, per_piece - 1), 0)

    return pl.pallas_call(
        functools.partial(laid_out_body, per_piece),
        grid=(rows // high,),
        in_specs=[
            pl.BlockSpec((high, parts, bins, taps), lambda i: (i, 0, 0, 0)),
            pl.BlockSpec((high, 1), lambda i: (i, 0)),
        ],
        out_specs=[pl.BlockSpec((high, width), lambda i: (i, 0))]
        + [pl.BlockSpec((high, width), place(piece)) for piece in range(pieces)],
        out_shape=[jax.ShapeDtypeStruct((rows, width), spectra.dtype)]
        + [jax.ShapeDtypeStruct((rows // pieces, width), spectra.dtype)] * pieces,
    )(spectra, flags.reshape(rows, 1))


def products_body(sizes, scale_coef, raw, plan_ref, *refs):
    shapes, at_once, known, units = sizes
    refs = list(refs)
    rows, at = [], 0
    for shape in shapes:
        rows.append(refs[at : at + len(shape)])
        at += len(shape)
    columns = refs[at : at + known]
    held, right, col_marks, staged, row_sems, col_sems, out_sems = refs[-7:]
    outs = refs[-9:-7] if raw else refs[-8:-7]
    unit, part = pl.program_id(0), pl.program_id(1)
    parts = len(rows) // at_once
    now = unit * parts + part
    shard_rows = held.shape[1] // at_once
    cols, half_width = right.shape[1] // 2, right.shape[2] // 2
    half_cols = cols // 2

    def row_copies(index, row, slot):
        copies, top = [], row * shard_rows
        for number, piece in enumerate(rows[index]):
            where = held.at[slot, pl.ds(top, piece.shape[0])]
            copies.append(pltpu.make_async_copy(piece, where, row_sems.at[slot, row, number]))
            top += piece.shape[0]
        return copies

    def start_rows(which, slot):
        for index in range(parts):

            @pl.when(which == index)
            def _():
                for row in range(at_once):
                    for copy in row_copies(index * at_once + row, row, slot):
                        copy.start()

    def col_copies(source, half, slot):
        top = half * half_cols
        real = source.at[:, pl.ds(0, half_width)]
        imag = source.at[:, pl.ds(half_width, half_width)]
        marks = source.at[:, pl.ds(2 * half_width, LANES)]
        places = [
            (real, right.at[slot, pl.ds(top, half_cols), pl.ds(0, half_width)]),
            (imag, right.at[slot, pl.ds(top, half_cols), pl.ds(half_width, half_width)]),
            (real, right.at[slot, pl.ds(cols + top, half_cols), pl.ds(half_width, half_width)]),
            (marks, col_marks.at[slot, pl.ds(top, half_cols)]),
        ]
        return [
            pltpu.make_async_copy(start, end, col_sems.at[slot, half, kind])
            for kind, (start, end) in enumerate(places)
        ]

    def start_cols(which, slot):
        for half in range(2):
            for index in range(known):

                @pl.when(plan_ref[2 * which + half] == index)
                def _():
                    for copy in col_copies(columns[index], half, slot):
                        copy.start()

    def out_copies(slot):
        copies = []
        for row in range(at_once):
            group = plan_ref[4 * units + part * at_once + row]
            for half in range(2):
                start = plan_ref[2 * units + 2 * unit + half] * half_cols
                lanes = pl.ds(pl.multiple_of(start, half_cols), half_cols)
                source = staged.at[slot, :, row, :, pl.ds(half * half_cols, half_cols)]
                target = outs[0].at[:, group, :, lanes]
                copies.append(pltpu.make_async_copy(source, target, out_sems.at[slot, row, half]))
        return copies

    slot, col_slot = lax.rem(now, 2), lax.rem(unit, 2)

    @pl.when(now == 0)
    def _():
        start_rows(0, 0)
        start_cols(0, 0)

    @pl.when(now + 1 < units * parts)
    def _():
        start_rows(lax.rem(part + 1, parts), lax.rem(now + 1, 2))

    @pl.when(jnp.logical_and(part == 0, unit + 1 < units))
    def _():
        start_cols(unit + 1, lax.rem(unit + 1, 2))

    @pl.when(part == 0)
    def _():
        for half in range(2):
            for copy in col_copies(columns[0], half, col_slot):
                copy.wait()
        right[col_slot, cols:, :half_width] = -right[col_slot, :cols, half_width:]

    for row in range(at_once):
        for copy in row_copies(row, row, slot):
            copy.wait()

    left = held[slot, :, : 2 * half_width]
    product = lax.dot_general(left, right[col_slot], NT, preferred_element_type=jnp.float32)

    @pl.when(now >= 2)
    def _():
        for copy in out_copies(slot):
            copy.wait()

    def sums(values, axis):
        def one(first):
            take = [lax.slice_in_dim(values, i, i + 1, axis=axis) for i in range(first, first + 3)]
            return (take[2] + take[1]) + take[0]

        return one(0), one(3)

    col_factor, col_norm = sums(col_marks[col_slot].astype(jnp.float32).T, 0)
    for row in range(at_once):
        top = row * shard_rows
        marks = held[slot, pl.ds(top, shard_rows), pl.ds(2 * half_width, LANES)]
        row_factor, row_norm = sums(marks.astype(jnp.float32), 1)
        scaling = (row_factor * scale_coef) * col_factor
        if raw:
            bound = jnp.max(row_factor / row_norm, axis=0, keepdims=True)
            bound = bound * jnp.max(col_factor / col_norm, axis=1, keepdims=True)
            unit_size = jnp.maximum(bound * (2 * half_width * scale_coef), FLOOR) / 32768
            group = plan_ref[4 * units + part * at_once + row]
            outs[1][group] = jnp.broadcast_to(unit_size, outs[1].shape[1:])
            scaling = scaling * (1 / unit_size)
        staged[slot, 0, row] = product[top : top + shard_rows, :cols] * scaling
        staged[slot, 1, row] = product[top : top + shard_rows, cols:] * scaling

    for copy in out_copies(slot):
        copy.start()

    @pl.when(now == units * parts - 1)
    def _():
        for copy in out_copies(lax.rem(now + 1, 2)) + out_copies(slot):
            copy.wait()


def plan_of(choice, slots, groups):
    return jnp.stack(list(choice) + list(slots) + list(groups)).astype(jnp.int32)


def products(out, rows, columns, plan, blocks, scale_coef, raw=False):
    shard_rows = sum(piece.shape[0] for piece in rows[0])
    width = rows[0][0].shape[1]
    half_width = (width - LANES) // 2
    count = len(rows)
    units = (plan.shape[0] - count) // 4
    at_once = 2 if units > 1 and count > 1 else 1
    parts = count // at_once
    cols = 2 * columns[0].shape[0]
    whole = pl.BlockSpec(memory_space=pl.ANY)
    operands = [piece for pieces in rows for piece in pieces] + list(columns)
    aliases = {}
    if out is not None:
        aliases = {1 + len(operands): 0}
        operands.append(out)
    shape = (2, count, shard_rows, cols if raw else shard_rows * blocks)
    out_shape = [jax.ShapeDtypeStruct(shape, jnp.float32)]
    out_specs = [whole]
    if raw:
        out_shape.append(jax.ShapeDtypeStruct((count, 8, LANES), jnp.float32))
        out_specs.append(
            pl.BlockSpec((count, 8, LANES), lambda i, j, s: (0, 0, 0))
        )
    shapes = [[piece.shape[0] for piece in pieces] for pieces in rows]
    most = max(len(pieces) for pieces in rows)
    given = pl.pallas_call(
        functools.partial(products_body, (shapes, at_once, len(columns), units), scale_coef, raw),
        grid_spec=pltpu.PrefetchScalarGridSpec(
            num_scalar_prefetch=1,
            grid=(units, parts),
            in_specs=[whole] * len(operands),
            out_specs=out_specs,
            scratch_shapes=[
                pltpu.VMEM((2, at_once * shard_rows, width), rows[0][0].dtype),
                pltpu.VMEM((2, 2 * cols, 2 * half_width), rows[0][0].dtype),
                pltpu.VMEM((2, cols, LANES), rows[0][0].dtype),
                pltpu.VMEM((2, 2, at_once, shard_rows, cols), jnp.float32),
                pltpu.SemaphoreType.DMA((2, at_once, most)),
                pltpu.SemaphoreType.DMA((2, 2, 4)),
                pltpu.SemaphoreType.DMA((2, at_once, 2)),
            ],
        ),
        out_shape=out_shape,
        input_output_aliases=aliases,
        cost_estimate=pl.CostEstimate(
            flops=8 * units * count * shard_rows * cols * half_width,
            bytes_accessed=4 * units * half_width * (count * shard_rows + cols),
            transcendentals=0,
        ),
        compiler_params=pltpu.CompilerParams(
            dimension_semantics=("arbitrary", "arbitrary"), vmem_limit_bytes=60 * 2**20
        ),
    )(plan, *operands)
    return given if raw else given[0]


def gathered(spectra, detector_valid, scale_coef):
    shard_rows = spectra.shape[1]
    half_width = spectra.shape[3] * spectra.shape[4]
    flattened = spectra.reshape(shard_rows, 2 * half_width)
    widened = flattened.astype(jnp.float32)
    power_mean = jnp.mean(widened * widened, axis=1) + 1e-06
    own_factor = detector_valid.reshape(shard_rows).astype(jnp.float32) * lax.rsqrt(power_mean)
    rows = lax.all_gather(flattened, "grp", axis=0, tiled=True)
    cols = lax.all_gather(flattened, "blk", axis=0, tiled=True)
    row_factor = lax.all_gather(own_factor, "grp", axis=0, tiled=True) * scale_coef
    col_factor = lax.all_gather(own_factor, "blk", axis=0, tiled=True)
    rotated = jnp.concatenate([-cols[:, half_width:], cols[:, :half_width]], axis=1)
    scaling = row_factor[:, None] * col_factor[None, :]
    parts = [
        lax.dot_general(rows, right, NT, preferred_element_type=jnp.float32) * scaling
        for right in (cols, rotated)
    ]
    return jnp.stack(parts)


def shards(spectra, detector_valid):
    shard_rows = spectra.shape[1]
    half_width = spectra.shape[3] * spectra.shape[4]
    blocks = lax.axis_size("blk")
    group_size = lax.axis_size("grp")
    scale_coef = 0.5 / math.sqrt(half_width)
    shape = (2, group_size, shard_rows, blocks * shard_rows)
    fits = shard_rows % 256 == 0 and half_width % 128 == 0 and group_size & (group_size - 1) == 0
    if blocks != 8 or group_size < 2 or not fits:
        return gathered(spectra, detector_valid, scale_coef).reshape(shape)

    devices = range(blocks)
    inner = [b for b in devices if 0 < b // 2 < blocks // 2 - 1]
    ends = [b for b in devices if b not in inner]
    me = lax.axis_index("blk")
    mine = lax.axis_index("grp")
    is_end = jnp.logical_or(me // 2 == 0, me // 2 == blocks // 2 - 1)

    def moved(value, axis, route):
        if not isinstance(value, tuple):
            return lax.ppermute(value, axis, route)
        pieces = []
        for piece in value:
            pieces.append(lax.ppermute(piece, axis, route))
        return tuple(pieces)

    def swap(value, among, by):
        return moved(value, "blk", [(b, b ^ by) for b in among])

    def spread(value, by):
        return moved(value, "grp", [(g, g ^ by) for g in range(group_size)])

    def begun(value):
        return {0: value, group_size // 2: spread(value, group_size // 2)}

    def finished(arrays):
        by = group_size // 4
        while by:
            arrays = arrays | {key ^ by: spread(array, by) for key, array in arrays.items()}
            by //= 2
        return [arrays[key] for key in range(group_size)]

    def held_for(value, *after):
        return tied(value, *after)[0]

    def either(inner_value, end_value):
        return jnp.where(is_end, end_value, inner_value)

    groups = [mine ^ j for j in range(group_size)]

    def planned(units):
        choice, slots = [], []
        for inner_half, end_half in units:
            choice.append(either(*(2 * c + h for c, h, _ in (inner_half, end_half))))
            slots.append(either(*(2 * (me ^ slot) + h for _, h, slot in (inner_half, end_half))))
        return plan_of(choice, slots, groups)

    def put(out, columns, plan):
        halves = [half for column in columns for half in column]
        return products(out, rows, halves, plan, blocks, scale_coef)

    def both(inner_column, inner_slot, end_column, end_slot):
        return [((inner_column, h, inner_slot), (end_column, h, end_slot)) for h in (0, 1)]

    whole, *own = laid_out(spectra[0], detector_valid[0], 2)
    own = tuple(own)
    near = swap(own, devices, 2)
    beside = swap(own, devices, 1)
    across = swap(own, inner, 6)
    rows = begun(whole)
    last = group_size // 2
    rows[last] = held_for(rows[last], *near, *beside, *across)
    rows = [(array,) for array in finished(rows)]

    far_end = swap(near, inner, 6)
    end_beside = swap(beside, ends, 2)
    far_inner = swap(across, inner, 2)
    across_beside = swap(across, inner, 1)
    near_beside = swap(near, ends, 1)
    client = begun(near)

    zero = me * 0
    plans = [
        planned(both(0, 0, 0, 0) + both(1, 2, 1, 2) + both(2, 1, 2, 1) + both(3, 6, 0, 5)),
        planned([((0, 0, 4), (2, 0, 4)), ((1, 0, 3), (3, 0, 3))]),
        planned(both(0, 7, 3, 6) + [((1, 1, 4), (3, 1, 4)), ((2, 1, 3), (4, 1, 3))]),
        planned(both(0, 5, 1, 5)),
        plan_of([zero, zero + 1], [zero, zero + 1], groups),
    ]
    plan_a, plan_b, plan_c, plan_d, plan_served = passed(plans)
    out = put(
        None,
        [own, near, beside, across],
        plan_a,
    )
    *held, first_out = tied(far_end[0], far_inner[0], client[last][0], out)
    low = swap(held[0], inner, 1)
    low_beside = swap(held[1], ends, 1)
    firsts = finished({0: near[0], last: held[2]})
    out = put(
        first_out,
        [far_end[:1] * 2, end_beside[:1] * 2, far_inner[:1] * 2, near_beside[:1] * 2],
        plan_b,
    )
    *held, out = tied(end_beside[1], across_beside[1], client[last][1], out)
    high = swap(held[0], inner, 6)
    high_beside = swap(held[1], inner, 2)
    seconds = finished({0: near[1], last: held[2]})
    client = list(zip(firsts, seconds))

    def serve(columns):
        return products(None, client, columns, plan_served, blocks, scale_coef, raw=True)

    def deliver(block, unit_size):
        return swap(block.astype(jnp.float16), inner, 2), swap(unit_size, inner, 2)

    def place(out, sent, end_slot):
        block, unit_size = sent
        block = block.astype(jnp.float32) * unit_size[None, :, :1, :1]
        start = (me ^ end_slot) * shard_rows
        starts = [jnp.zeros_like(start)] * 3 + [start]
        kept = lax.dynamic_slice(out, starts, block.shape)
        return lax.dynamic_update_slice(out, jnp.where(is_end, block, kept), starts)

    first = serve(far_end)
    sent_a = deliver(*first)
    out, _ = tied(out, first[1])
    out = put(
        out,
        [across_beside, far_end, end_beside, far_inner, near_beside],
        plan_c,
    )
    low, high, low_beside, high_beside, out = tied(low, high, low_beside, high_beside, out)
    second = serve((low, high))
    sent_b = deliver(*second)
    out, _ = tied(out, second[1])
    out = put(out, [(low, high), (low_beside, high_beside)], plan_d)
    out = place(out, sent_a, 6)
    out = place(out, sent_b, 7)
    return out.reshape(shape)


def solution(mesh):
    return jax.shard_map(
        shards,
        mesh=mesh,
        in_specs=(P("grp", "blk", None, None, None), P("grp", "blk")),
        out_specs=P(None, None, "blk", "grp"),
        check_vma=False,
    )
```

```python
import functools
import math

import jax
import jax.numpy as jnp
from jax import lax
from jax.experimental import pallas as pl
from jax.experimental.pallas import tpu as pltpu
from jax.sharding import PartitionSpec as P


NT = (((1,), (1,)), ((), ()))
LANES = 128
FLOOR = 1e-30


def tile_of(size, most):
    tile = 1
    while tile * 2 <= most and size % (tile * 2) == 0:
        tile *= 2
    return tile


def passed_body(count, *refs):
    for value_ref, out_ref in zip(refs[:count], refs[count:]):
        out_ref[...] = value_ref[...]


def passed(values):
    return pl.pallas_call(
        functools.partial(passed_body, len(values)),
        out_shape=[jax.ShapeDtypeStruct(value.shape, value.dtype) for value in values],
    )(*values)


def tied(*values):
    return lax.optimization_barrier(values)


def split_in_three(value):
    parts = []
    for _ in range(2):
        part = value.astype(jnp.bfloat16).astype(jnp.float32)
        parts.append(part)
        value = value - part
    return parts + [value]


def laid_out_body(per_piece, spectra_ref, flags_ref, whole_ref, *piece_refs):
    high, parts, bins, taps = spectra_ref.shape
    half_width = bins * taps

    def fill(out_ref):
        power = jnp.zeros((high, 1), jnp.float32)
        for part in range(parts):
            flat = spectra_ref[:, part].reshape(high, half_width)
            out_ref[:, part * half_width : (part + 1) * half_width] = flat
            widened = flat.astype(jnp.float32)
            power = power + jnp.sum(widened * widened, axis=1, keepdims=True)
        power_mean = power / (parts * half_width)
        factor = flags_ref[...].astype(jnp.float32) * lax.rsqrt(power_mean + 1e-06)
        norm = lax.rsqrt(jnp.maximum(power_mean, FLOOR))
        lane = lax.broadcasted_iota(jnp.int32, (high, LANES), 1)
        marks = jnp.zeros((high, LANES), jnp.float32)
        for index, value in enumerate(split_in_three(factor) + split_in_three(norm)):
            marks = jnp.where(lane == index, value, marks)
        out_ref[:, parts * half_width :] = marks.astype(jnp.bfloat16)

    fill(whole_ref)
    for piece, out_ref in enumerate(piece_refs):

        @pl.when(pl.program_id(0) // per_piece == piece)
        def _():
            out_ref[...] = whole_ref[...]


def laid_out(spectra, flags, pieces):
    rows, parts, bins, taps = spectra.shape
    width = parts * bins * taps + LANES
    high = tile_of(rows // pieces, 64)
    per_piece = rows // pieces // high

    def place(piece):
        first = piece * per_piece
        return lambda i: (jnp.clip(i - first, 0, per_piece - 1), 0)

    return pl.pallas_call(
        functools.partial(laid_out_body, per_piece),
        grid=(rows // high,),
        in_specs=[
            pl.BlockSpec((high, parts, bins, taps), lambda i: (i, 0, 0, 0)),
            pl.BlockSpec((high, 1), lambda i: (i, 0)),
        ],
        out_specs=[pl.BlockSpec((high, width), lambda i: (i, 0))]
        + [pl.BlockSpec((high, width), place(piece)) for piece in range(pieces)],
        out_shape=[jax.ShapeDtypeStruct((rows, width), spectra.dtype)]
        + [jax.ShapeDtypeStruct((rows // pieces, width), spectra.dtype)] * pieces,
    )(spectra, flags.reshape(rows, 1))


def products_body(sizes, scale_coef, plan_ref, *refs):
    sets, at_once, known, units, served, given = sizes
    refs = list(refs)
    row_sets, at = [], 0
    for shapes in sets:
        rows = []
        for shape in shapes:
            rows.append(refs[at : at + len(shape)])
            at += len(shape)
        row_sets.append(rows)
    columns = refs[at : at + known]
    held, right, col_marks, staged, inverse, row_sems, col_sems, out_sems = refs[-8:]
    main = [] if served == units else [refs[at + known + given]]
    extra = refs[-10:-8] if served else []
    unit, part = pl.program_id(0), pl.program_id(1)
    parts = len(row_sets[0]) // at_once
    now = unit * parts + part
    shard_rows = held.shape[1] // at_once
    cols, half_width = right.shape[1] // 2, right.shape[2] // 2
    half_cols = cols // 2

    def for_set(which_unit, body):
        if len(row_sets) == 1:
            body(row_sets[0])
        else:
            pl.when(which_unit < served)(lambda: body(row_sets[1]))
            pl.when(which_unit >= served)(lambda: body(row_sets[0]))

    def row_copies(pieces, row, slot):
        copies, top = [], row * shard_rows
        for number, piece in enumerate(pieces):
            where = held.at[slot, pl.ds(top, piece.shape[0])]
            copies.append(pltpu.make_async_copy(piece, where, row_sems.at[slot, row, number]))
            top += piece.shape[0]
        return copies

    def start_rows(which_unit, which, slot):
        def start(rows):
            for index in range(parts):

                @pl.when(which == index)
                def _():
                    for row in range(at_once):
                        for copy in row_copies(rows[index * at_once + row], row, slot):
                            copy.start()

        for_set(which_unit, start)

    def wait_rows(rows):
        for row in range(at_once):
            for copy in row_copies(rows[row], row, slot):
                copy.wait()

    def col_copies(source, half, slot):
        top = half * half_cols
        real = source.at[:, pl.ds(0, half_width)]
        imag = source.at[:, pl.ds(half_width, half_width)]
        marks = source.at[:, pl.ds(2 * half_width, LANES)]
        places = [
            (real, right.at[slot, pl.ds(top, half_cols), pl.ds(0, half_width)]),
            (imag, right.at[slot, pl.ds(top, half_cols), pl.ds(half_width, half_width)]),
            (real, right.at[slot, pl.ds(cols + top, half_cols), pl.ds(half_width, half_width)]),
            (marks, col_marks.at[slot, pl.ds(top, half_cols)]),
        ]
        return [
            pltpu.make_async_copy(start, end, col_sems.at[slot, half, kind])
            for kind, (start, end) in enumerate(places)
        ]

    def start_cols(which, slot):
        for half in range(2):
            for index in range(known):

                @pl.when(plan_ref[2 * which + half] == index)
                def _():
                    for copy in col_copies(columns[index], half, slot):
                        copy.start()

    def out_copies(slot, target_ref=None):
        target_ref = (main + extra)[0] if target_ref is None else target_ref
        copies = []
        for row in range(at_once):
            group = plan_ref[4 * units + part * at_once + row]
            for half in range(2):
                start = plan_ref[2 * units + 2 * unit + half] * half_cols
                lanes = pl.ds(pl.multiple_of(start, half_cols), half_cols)
                source = staged.at[slot, :, row, :, pl.ds(half * half_cols, half_cols)]
                target = target_ref.at[:, group, :, lanes]
                copies.append(pltpu.make_async_copy(source, target, out_sems.at[slot, row, half]))
        return copies

    slot, col_slot = lax.rem(now, 2), lax.rem(unit, 2)

    @pl.when(now == 0)
    def _():
        start_rows(0, 0, 0)
        start_cols(0, 0)

    @pl.when(now + 1 < units * parts)
    def _():
        start_rows(lax.div(now + 1, parts), lax.rem(part + 1, parts), lax.rem(now + 1, 2))

    @pl.when(jnp.logical_and(part == 0, unit + 1 < units))
    def _():
        start_cols(unit + 1, lax.rem(unit + 1, 2))

    @pl.when(part == 0)
    def _():
        for half in range(2):
            for copy in col_copies(columns[0], half, col_slot):
                copy.wait()
        right[col_slot, cols:, :half_width] = -right[col_slot, :cols, half_width:]

    for_set(unit, wait_rows)
    left = held[slot, :, : 2 * half_width]
    product = lax.dot_general(left, right[col_slot], NT, preferred_element_type=jnp.float32)

    @pl.when(now >= 2)
    def _():
        for copy in out_copies(slot):
            copy.wait()

    def sums(values, axis):
        def one(first):
            take = [lax.slice_in_dim(values, i, i + 1, axis=axis) for i in range(first, first + 3)]
            return (take[2] + take[1]) + take[0]

        return one(0), one(3)

    col_factor, col_norm = sums(col_marks[col_slot].astype(jnp.float32).T, 0)
    for row in range(at_once):
        top = row * shard_rows
        marks = held[slot, pl.ds(top, shard_rows), pl.ds(2 * half_width, LANES)]
        row_factor, row_norm = sums(marks.astype(jnp.float32), 1)
        scaling = (row_factor * scale_coef) * col_factor
        if served:

            @pl.when(unit < served)
            def _():
                bound = jnp.max(row_factor / row_norm, axis=0, keepdims=True)
                bound = bound * jnp.max(col_factor / col_norm, axis=1, keepdims=True)
                unit_size = jnp.maximum(bound * (2 * half_width * scale_coef), FLOOR) / 32768
                group = plan_ref[4 * units + part * at_once + row]
                extra[1][group] = jnp.broadcast_to(unit_size, extra[1].shape[1:])
                inverse[...] = jnp.broadcast_to(1 / unit_size, inverse.shape)

            if main:

                @pl.when(unit >= served)
                def _():
                    inverse[...] = jnp.ones_like(inverse)

            scaling = scaling * inverse[0:1, 0:1]
        staged[slot, 0, row] = product[top : top + shard_rows, :cols] * scaling
        staged[slot, 1, row] = product[top : top + shard_rows, cols:] * scaling

    def start_out(target_ref):
        for copy in out_copies(slot, target_ref):
            copy.start()

    if served and main:
        pl.when(unit < served)(lambda: start_out(extra[0]))
        pl.when(unit >= served)(lambda: start_out(main[0]))
    else:
        start_out((main + extra)[0])

    @pl.when(now == units * parts - 1)
    def _():
        for copy in out_copies(lax.rem(now + 1, 2)) + out_copies(slot):
            copy.wait()


def plan_of(choice, slots, groups):
    return jnp.stack(list(choice) + list(slots) + list(groups)).astype(jnp.int32)


def products(out, row_sets, columns, plan, blocks, scale_coef, served=0):
    count = len(row_sets[0])
    units = (plan.shape[0] - count) // 4
    shard_rows = sum(piece.shape[0] for piece in row_sets[0][0])
    width = row_sets[0][0][0].shape[1]
    kind = row_sets[0][0][0].dtype
    half_width = (width - LANES) // 2
    at_once = 2 if units > 1 and count > 1 else 1
    parts = count // at_once
    cols = 2 * columns[0].shape[0]
    whole = pl.BlockSpec(memory_space=pl.ANY)
    operands = [piece for rows in row_sets for pieces in rows for piece in pieces]
    operands += list(columns)
    aliases = {}
    if out is not None:
        aliases = {1 + len(operands): 0}
        operands.append(out)
    out_shape, out_specs = [], []
    if served < units:
        shape = (2, count, shard_rows, shard_rows * blocks)
        out_shape.append(jax.ShapeDtypeStruct(shape, jnp.float32))
        out_specs.append(whole)
    if served:
        sizes = (count, 8, LANES)
        out_shape.append(jax.ShapeDtypeStruct((2, count, shard_rows, cols), jnp.float32))
        out_shape.append(jax.ShapeDtypeStruct(sizes, jnp.float32))
        out_specs += [whole, pl.BlockSpec(sizes, lambda i, j, s: (0, 0, 0))]
    sets = [[[piece.shape[0] for piece in pieces] for pieces in rows] for rows in row_sets]
    most = max(len(pieces) for rows in row_sets for pieces in rows)
    sizes = (sets, at_once, len(columns), units, served, int(out is not None))
    return pl.pallas_call(
        functools.partial(products_body, sizes, scale_coef),
        grid_spec=pltpu.PrefetchScalarGridSpec(
            num_scalar_prefetch=1,
            grid=(units, parts),
            in_specs=[whole] * len(operands),
            out_specs=out_specs,
            scratch_shapes=[
                pltpu.VMEM((2, at_once * shard_rows, width), kind),
                pltpu.VMEM((2, 2 * cols, 2 * half_width), kind),
                pltpu.VMEM((2, cols, LANES), kind),
                pltpu.VMEM((2, 2, at_once, shard_rows, cols), jnp.float32),
                pltpu.VMEM((8, LANES), jnp.float32),
                pltpu.SemaphoreType.DMA((2, at_once, most)),
                pltpu.SemaphoreType.DMA((2, 2, 4)),
                pltpu.SemaphoreType.DMA((2, at_once, 2)),
            ],
        ),
        out_shape=out_shape,
        input_output_aliases=aliases,
        cost_estimate=pl.CostEstimate(
            flops=8 * units * count * shard_rows * cols * half_width,
            bytes_accessed=4 * units * half_width * (count * shard_rows + cols),
            transcendentals=0,
        ),
        compiler_params=pltpu.CompilerParams(
            dimension_semantics=("arbitrary", "arbitrary"), vmem_limit_bytes=60 * 2**20
        ),
    )(plan, *operands)


def gathered(spectra, detector_valid, scale_coef):
    shard_rows = spectra.shape[1]
    half_width = spectra.shape[3] * spectra.shape[4]
    flattened = spectra.reshape(shard_rows, 2 * half_width)
    widened = flattened.astype(jnp.float32)
    power_mean = jnp.mean(widened * widened, axis=1) + 1e-06
    own_factor = detector_valid.reshape(shard_rows).astype(jnp.float32) * lax.rsqrt(power_mean)
    rows = lax.all_gather(flattened, "grp", axis=0, tiled=True)
    cols = lax.all_gather(flattened, "blk", axis=0, tiled=True)
    row_factor = lax.all_gather(own_factor, "grp", axis=0, tiled=True) * scale_coef
    col_factor = lax.all_gather(own_factor, "blk", axis=0, tiled=True)
    rotated = jnp.concatenate([-cols[:, half_width:], cols[:, :half_width]], axis=1)
    scaling = row_factor[:, None] * col_factor[None, :]
    parts = [
        lax.dot_general(rows, right, NT, preferred_element_type=jnp.float32) * scaling
        for right in (cols, rotated)
    ]
    return jnp.stack(parts)


def shards(spectra, detector_valid):
    shard_rows = spectra.shape[1]
    half_width = spectra.shape[3] * spectra.shape[4]
    blocks = lax.axis_size("blk")
    group_size = lax.axis_size("grp")
    scale_coef = 0.5 / math.sqrt(half_width)
    shape = (2, group_size, shard_rows, blocks * shard_rows)
    fits = shard_rows % 256 == 0 and half_width % 128 == 0 and group_size & (group_size - 1) == 0
    if blocks != 8 or group_size < 2 or not fits:
        return gathered(spectra, detector_valid, scale_coef).reshape(shape)

    devices = range(blocks)
    inner = [b for b in devices if 0 < b // 2 < blocks // 2 - 1]
    ends = [b for b in devices if b not in inner]
    me = lax.axis_index("blk")
    mine = lax.axis_index("grp")
    is_end = jnp.logical_or(me // 2 == 0, me // 2 == blocks // 2 - 1)

    def moved(value, axis, route):
        if not isinstance(value, tuple):
            return lax.ppermute(value, axis, route)
        pieces = []
        for piece in value:
            pieces.append(lax.ppermute(piece, axis, route))
        return tuple(pieces)

    def swap(value, among, by):
        return moved(value, "blk", [(b, b ^ by) for b in among])

    def spread(value, by):
        return moved(value, "grp", [(g, g ^ by) for g in range(group_size)])

    def begun(value):
        return {0: value, group_size // 2: spread(value, group_size // 2)}

    def finished(arrays):
        by = group_size // 4
        while by:
            arrays = arrays | {key ^ by: spread(array, by) for key, array in arrays.items()}
            by //= 2
        return [arrays[key] for key in range(group_size)]

    def held_for(value, *after):
        return tied(value, *after)[0]

    def either(inner_value, end_value):
        return jnp.where(is_end, end_value, inner_value)

    groups = [mine ^ j for j in range(group_size)]

    def planned(units, served=()):
        choice, slots = list(served), [me * 0, me * 0 + 1][: len(served)]
        for inner_half, end_half in units:
            choice.append(either(*(2 * c + h for c, h, _ in (inner_half, end_half))))
            slots.append(either(*(2 * (me ^ slot) + h for _, h, slot in (inner_half, end_half))))
        return plan_of(choice, slots, groups)

    def put(out, columns, plan):
        halves = [half for column in columns for half in column]
        return products(out, [rows], halves, plan, blocks, scale_coef)[0]

    def both(inner_column, inner_slot, end_column, end_slot):
        return [((inner_column, h, inner_slot), (end_column, h, end_slot)) for h in (0, 1)]

    whole, *own = laid_out(spectra[0], detector_valid[0], 2)
    own = tuple(own)
    near = swap(own, devices, 2)
    beside = swap(own, devices, 1)
    across = swap(own, inner, 6)
    rows = begun(whole)
    last = group_size // 2
    rows[last] = held_for(rows[last], *near, *beside, *across)
    rows = [(array,) for array in finished(rows)]

    far_end = swap(near, inner, 6)
    end_beside = swap(beside, ends, 2)
    far_inner = swap(across, inner, 2)
    across_beside = swap(across, inner, 1)
    near_beside = swap(near, ends, 1)
    client = begun(near)

    zero, one = me * 0, me * 0 + 1
    units_c = both(0, 7, 3, 6) + [((1, 1, 4), (3, 1, 4)), ((2, 1, 3), (4, 1, 3))]
    plan_c = planned(units_c, [zero + 2, zero + 3])
    plans = [
        planned(both(0, 0, 0, 0) + both(1, 2, 1, 2) + both(2, 1, 2, 1) + both(3, 6, 0, 5)),
        planned([((0, 0, 4), (2, 0, 4)), ((1, 0, 3), (3, 0, 3))]),
        plan_c,
        planned(both(0, 5, 1, 5)),
        plan_of([zero, one], [zero, one], groups),
    ]
    plan_a, plan_b, plan_c, plan_d, plan_served = passed(plans)
    out = put(
        None,
        [own, near, beside, across],
        plan_a,
    )
    *held, first_out = tied(far_end[0], far_inner[0], client[last][0], out)
    low = swap(held[0], inner, 1)
    low_beside = swap(held[1], ends, 1)
    firsts = finished({0: near[0], last: held[2]})
    out = put(
        first_out,
        [far_end[:1] * 2, end_beside[:1] * 2, far_inner[:1] * 2, near_beside[:1] * 2],
        plan_b,
    )
    *held, out = tied(end_beside[1], across_beside[1], client[last][1], out)
    high = swap(held[0], inner, 6)
    high_beside = swap(held[1], inner, 2)
    seconds = finished({0: near[1], last: held[2]})
    client = list(zip(firsts, seconds))

    def deliver(block, unit_size):
        return swap(block.astype(jnp.float16), inner, 2), swap(unit_size, inner, 2)

    def place(out, sent, end_slot):
        block, unit_size = sent
        block = block.astype(jnp.float32) * unit_size[None, :, :1, :1]
        start = (me ^ end_slot) * shard_rows
        starts = [jnp.zeros_like(start)] * 3 + [start]
        kept = lax.dynamic_slice(out, starts, block.shape)
        return lax.dynamic_update_slice(out, jnp.where(is_end, block, kept), starts)

    columns = [across_beside, far_end, end_beside, far_inner, near_beside]
    out, *first = products(
        out,
        [rows, client],
        [half for column in columns for half in column],
        plan_c,
        blocks,
        scale_coef,
        served=1,
    )
    sent_a = deliver(*first)
    low, high, low_beside, high_beside, out = tied(low, high, low_beside, high_beside, out)
    second = products(None, [client], [low, high], plan_served, blocks, scale_coef, served=1)
    sent_b = deliver(*second)
    out, _ = tied(out, second[1])
    out = put(out, [(low, high), (low_beside, high_beside)], plan_d)
    out = place(out, sent_a, 6)
    out = place(out, sent_b, 7)
    return out.reshape(shape)


def solution(mesh):
    return jax.shard_map(
        shards,
        mesh=mesh,
        in_specs=(P("grp", "blk", None, None, None), P("grp", "blk")),
        out_specs=P(None, None, "blk", "grp"),
        check_vma=False,
    )
```

```python
import functools
import math

import jax
import jax.numpy as jnp
from jax import lax
from jax.experimental import pallas as pl
from jax.experimental.pallas import tpu as pltpu
from jax.sharding import PartitionSpec as P


NT = (((1,), (1,)), ((), ()))
LANES = 128
FLOOR = 1e-30


def tile_of(size, most):
    tile = 1
    while tile * 2 <= most and size % (tile * 2) == 0:
        tile *= 2
    return tile


def passed_body(count, *refs):
    for value_ref, out_ref in zip(refs[:count], refs[count:]):
        out_ref[...] = value_ref[...]


def passed(values):
    return pl.pallas_call(
        functools.partial(passed_body, len(values)),
        out_shape=[jax.ShapeDtypeStruct(value.shape, value.dtype) for value in values],
    )(*values)


def tied(*values):
    return lax.optimization_barrier(values)


def split_in_three(value):
    parts = []
    for _ in range(2):
        part = value.astype(jnp.bfloat16).astype(jnp.float32)
        parts.append(part)
        value = value - part
    return parts + [value]


def laid_out_body(per_piece, spectra_ref, flags_ref, whole_ref, *piece_refs):
    high, parts, bins, taps = spectra_ref.shape
    half_width = bins * taps

    def fill(out_ref):
        power = jnp.zeros((high, 1), jnp.float32)
        for part in range(parts):
            flat = spectra_ref[:, part].reshape(high, half_width)
            out_ref[:, part * half_width : (part + 1) * half_width] = flat
            widened = flat.astype(jnp.float32)
            power = power + jnp.sum(widened * widened, axis=1, keepdims=True)
        power_mean = power / (parts * half_width)
        factor = flags_ref[...].astype(jnp.float32) * lax.rsqrt(power_mean + 1e-06)
        norm = lax.rsqrt(jnp.maximum(power_mean, FLOOR))
        lane = lax.broadcasted_iota(jnp.int32, (high, LANES), 1)
        marks = jnp.zeros((high, LANES), jnp.float32)
        for index, value in enumerate(split_in_three(factor) + split_in_three(norm)):
            marks = jnp.where(lane == index, value, marks)
        out_ref[:, parts * half_width :] = marks.astype(jnp.bfloat16)

    fill(whole_ref)
    for piece, out_ref in enumerate(piece_refs):

        @pl.when(pl.program_id(0) // per_piece == piece)
        def _():
            out_ref[...] = whole_ref[...]


def laid_out(spectra, flags, pieces):
    rows, parts, bins, taps = spectra.shape
    width = parts * bins * taps + LANES
    high = tile_of(rows // pieces, 64)
    per_piece = rows // pieces // high

    def place(piece):
        first = piece * per_piece
        return lambda i: (jnp.clip(i - first, 0, per_piece - 1), 0)

    return pl.pallas_call(
        functools.partial(laid_out_body, per_piece),
        grid=(rows // high,),
        in_specs=[
            pl.BlockSpec((high, parts, bins, taps), lambda i: (i, 0, 0, 0)),
            pl.BlockSpec((high, 1), lambda i: (i, 0)),
        ],
        out_specs=[pl.BlockSpec((high, width), lambda i: (i, 0))]
        + [pl.BlockSpec((high, width), place(piece)) for piece in range(pieces)],
        out_shape=[jax.ShapeDtypeStruct((rows, width), spectra.dtype)]
        + [jax.ShapeDtypeStruct((rows // pieces, width), spectra.dtype)] * pieces,
    )(spectra, flags.reshape(rows, 1))


def products_body(sizes, scale_coef, plan_ref, *refs):
    sets, at_once, known, units, served, given = sizes
    refs = list(refs)
    row_sets, at = [], 0
    for shapes in sets:
        rows = []
        for shape in shapes:
            rows.append(refs[at : at + len(shape)])
            at += len(shape)
        row_sets.append(rows)
    columns = refs[at : at + known]
    held, right, col_marks, staged, inverse, row_sems, col_sems, out_sems = refs[-8:]
    main = [] if served == units else [refs[at + known + given]]
    extra = refs[-10:-8] if served else []
    unit, part = pl.program_id(0), pl.program_id(1)
    parts = len(row_sets[0]) // at_once
    now = unit * parts + part
    shard_rows = held.shape[1] // at_once
    cols, half_width = right.shape[1] // 2, right.shape[2] // 2
    half_cols = cols // 2

    def for_set(which_unit, body):
        if len(row_sets) == 1:
            body(row_sets[0])
        else:
            pl.when(which_unit < served)(lambda: body(row_sets[1]))
            pl.when(which_unit >= served)(lambda: body(row_sets[0]))

    def row_copies(pieces, row, slot):
        copies, top = [], row * shard_rows
        for number, piece in enumerate(pieces):
            where = held.at[slot, pl.ds(top, piece.shape[0])]
            copies.append(pltpu.make_async_copy(piece, where, row_sems.at[slot, row, number]))
            top += piece.shape[0]
        return copies

    def start_rows(which_unit, which, slot):
        def start(rows):
            for index in range(parts):

                @pl.when(which == index)
                def _():
                    for row in range(at_once):
                        for copy in row_copies(rows[index * at_once + row], row, slot):
                            copy.start()

        for_set(which_unit, start)

    def wait_rows(rows):
        for row in range(at_once):
            for copy in row_copies(rows[row], row, slot):
                copy.wait()

    def col_copies(source, half, slot):
        top = half * half_cols
        real = source.at[:, pl.ds(0, half_width)]
        imag = source.at[:, pl.ds(half_width, half_width)]
        marks = source.at[:, pl.ds(2 * half_width, LANES)]
        places = [
            (real, right.at[slot, pl.ds(top, half_cols), pl.ds(0, half_width)]),
            (imag, right.at[slot, pl.ds(top, half_cols), pl.ds(half_width, half_width)]),
            (real, right.at[slot, pl.ds(cols + top, half_cols), pl.ds(half_width, half_width)]),
            (marks, col_marks.at[slot, pl.ds(top, half_cols)]),
        ]
        return [
            pltpu.make_async_copy(start, end, col_sems.at[slot, half, kind])
            for kind, (start, end) in enumerate(places)
        ]

    def start_cols(which, slot):
        for half in range(2):
            for index in range(known):

                @pl.when(plan_ref[2 * which + half] == index)
                def _():
                    for copy in col_copies(columns[index], half, slot):
                        copy.start()

    def out_copies(slot, target_ref=None):
        target_ref = (main + extra)[0] if target_ref is None else target_ref
        copies = []
        for row in range(at_once):
            group = plan_ref[4 * units + part * at_once + row]
            for half in range(2):
                start = plan_ref[2 * units + 2 * unit + half] * half_cols
                lanes = pl.ds(pl.multiple_of(start, half_cols), half_cols)
                source = staged.at[slot, :, row, :, pl.ds(half * half_cols, half_cols)]
                target = target_ref.at[:, group, :, lanes]
                copies.append(pltpu.make_async_copy(source, target, out_sems.at[slot, row, half]))
        return copies

    slot, col_slot = lax.rem(now, 2), lax.rem(unit, 2)

    @pl.when(now == 0)
    def _():
        start_rows(0, 0, 0)
        start_cols(0, 0)

    @pl.when(now + 1 < units * parts)
    def _():
        start_rows(lax.div(now + 1, parts), lax.rem(part + 1, parts), lax.rem(now + 1, 2))

    @pl.when(jnp.logical_and(part == 0, unit + 1 < units))
    def _():
        start_cols(unit + 1, lax.rem(unit + 1, 2))

    @pl.when(part == 0)
    def _():
        for half in range(2):
            for copy in col_copies(columns[0], half, col_slot):
                copy.wait()
        right[col_slot, cols:, :half_width] = -right[col_slot, :cols, half_width:]

    for_set(unit, wait_rows)
    left = held[slot, :, : 2 * half_width]
    product = lax.dot_general(left, right[col_slot], NT, preferred_element_type=jnp.float32)

    @pl.when(now >= 2)
    def _():
        for copy in out_copies(slot):
            copy.wait()

    def sums(values, axis):
        def one(first):
            take = [lax.slice_in_dim(values, i, i + 1, axis=axis) for i in range(first, first + 3)]
            return (take[2] + take[1]) + take[0]

        return one(0), one(3)

    col_factor, col_norm = sums(col_marks[col_slot].astype(jnp.float32).T, 0)
    for row in range(at_once):
        top = row * shard_rows
        marks = held[slot, pl.ds(top, shard_rows), pl.ds(2 * half_width, LANES)]
        row_factor, row_norm = sums(marks.astype(jnp.float32), 1)
        scaling = (row_factor * scale_coef) * col_factor
        if served:

            @pl.when(unit < served)
            def _():
                bound = jnp.max(row_factor / row_norm, axis=0, keepdims=True)
                bound = bound * jnp.max(col_factor / col_norm, axis=1, keepdims=True)
                unit_size = jnp.maximum(bound * (2 * half_width * scale_coef), FLOOR) / 32768
                group = plan_ref[4 * units + part * at_once + row]
                extra[1][group] = jnp.broadcast_to(unit_size, extra[1].shape[1:])
                inverse[...] = jnp.broadcast_to(1 / unit_size, inverse.shape)

            if main:

                @pl.when(unit >= served)
                def _():
                    inverse[...] = jnp.ones_like(inverse)

            scaling = scaling * inverse[0:1, 0:1]
        staged[slot, 0, row] = product[top : top + shard_rows, :cols] * scaling
        staged[slot, 1, row] = product[top : top + shard_rows, cols:] * scaling

    def start_out(target_ref):
        for copy in out_copies(slot, target_ref):
            copy.start()

    if served and main:
        pl.when(unit < served)(lambda: start_out(extra[0]))
        pl.when(unit >= served)(lambda: start_out(main[0]))
    else:
        start_out((main + extra)[0])

    @pl.when(now == units * parts - 1)
    def _():
        for copy in out_copies(lax.rem(now + 1, 2)) + out_copies(slot):
            copy.wait()


def plan_of(choice, slots, groups):
    return jnp.stack(list(choice) + list(slots) + list(groups)).astype(jnp.int32)


def products(out, row_sets, columns, plan, blocks, scale_coef, served=0):
    count = len(row_sets[0])
    units = (plan.shape[0] - count) // 4
    shard_rows = sum(piece.shape[0] for piece in row_sets[0][0])
    width = row_sets[0][0][0].shape[1]
    kind = row_sets[0][0][0].dtype
    half_width = (width - LANES) // 2
    at_once = 2 if units > 1 and count > 1 else 1
    parts = count // at_once
    cols = 2 * columns[0].shape[0]
    whole = pl.BlockSpec(memory_space=pl.ANY)
    operands = [piece for rows in row_sets for pieces in rows for piece in pieces]
    operands += list(columns)
    aliases = {}
    if out is not None:
        aliases = {1 + len(operands): 0}
        operands.append(out)
    out_shape, out_specs = [], []
    if served < units:
        shape = (2, count, shard_rows, shard_rows * blocks)
        out_shape.append(jax.ShapeDtypeStruct(shape, jnp.float32))
        out_specs.append(whole)
    if served:
        sizes = (count, 8, LANES)
        out_shape.append(jax.ShapeDtypeStruct((2, count, shard_rows, cols), jnp.float32))
        out_shape.append(jax.ShapeDtypeStruct(sizes, jnp.float32))
        out_specs += [whole, pl.BlockSpec(sizes, lambda i, j, s: (0, 0, 0))]
    sets = [[[piece.shape[0] for piece in pieces] for pieces in rows] for rows in row_sets]
    most = max(len(pieces) for rows in row_sets for pieces in rows)
    sizes = (sets, at_once, len(columns), units, served, int(out is not None))
    return pl.pallas_call(
        functools.partial(products_body, sizes, scale_coef),
        grid_spec=pltpu.PrefetchScalarGridSpec(
            num_scalar_prefetch=1,
            grid=(units, parts),
            in_specs=[whole] * len(operands),
            out_specs=out_specs,
            scratch_shapes=[
                pltpu.VMEM((2, at_once * shard_rows, width), kind),
                pltpu.VMEM((2, 2 * cols, 2 * half_width), kind),
                pltpu.VMEM((2, cols, LANES), kind),
                pltpu.VMEM((2, 2, at_once, shard_rows, cols), jnp.float32),
                pltpu.VMEM((8, LANES), jnp.float32),
                pltpu.SemaphoreType.DMA((2, at_once, most)),
                pltpu.SemaphoreType.DMA((2, 2, 4)),
                pltpu.SemaphoreType.DMA((2, at_once, 2)),
            ],
        ),
        out_shape=out_shape,
        input_output_aliases=aliases,
        cost_estimate=pl.CostEstimate(
            flops=8 * units * count * shard_rows * cols * half_width,
            bytes_accessed=4 * units * half_width * (count * shard_rows + cols),
            transcendentals=0,
        ),
        compiler_params=pltpu.CompilerParams(
            dimension_semantics=("arbitrary", "arbitrary"), vmem_limit_bytes=60 * 2**20
        ),
    )(plan, *operands)


def gathered(spectra, detector_valid, scale_coef):
    shard_rows = spectra.shape[1]
    half_width = spectra.shape[3] * spectra.shape[4]
    flattened = spectra.reshape(shard_rows, 2 * half_width)
    widened = flattened.astype(jnp.float32)
    power_mean = jnp.mean(widened * widened, axis=1) + 1e-06
    own_factor = detector_valid.reshape(shard_rows).astype(jnp.float32) * lax.rsqrt(power_mean)
    rows = lax.all_gather(flattened, "grp", axis=0, tiled=True)
    cols = lax.all_gather(flattened, "blk", axis=0, tiled=True)
    row_factor = lax.all_gather(own_factor, "grp", axis=0, tiled=True) * scale_coef
    col_factor = lax.all_gather(own_factor, "blk", axis=0, tiled=True)
    rotated = jnp.concatenate([-cols[:, half_width:], cols[:, :half_width]], axis=1)
    scaling = row_factor[:, None] * col_factor[None, :]
    parts = [
        lax.dot_general(rows, right, NT, preferred_element_type=jnp.float32) * scaling
        for right in (cols, rotated)
    ]
    return jnp.stack(parts)


def shards(spectra, detector_valid):
    shard_rows = spectra.shape[1]
    half_width = spectra.shape[3] * spectra.shape[4]
    blocks = lax.axis_size("blk")
    group_size = lax.axis_size("grp")
    scale_coef = 0.5 / math.sqrt(half_width)
    shape = (2, group_size, shard_rows, blocks * shard_rows)
    fits = shard_rows % 256 == 0 and half_width % 128 == 0 and group_size & (group_size - 1) == 0
    if blocks != 8 or group_size < 2 or not fits:
        return gathered(spectra, detector_valid, scale_coef).reshape(shape)

    devices = range(blocks)
    inner = [b for b in devices if 0 < b // 2 < blocks // 2 - 1]
    ends = [b for b in devices if b not in inner]
    me = lax.axis_index("blk")
    mine = lax.axis_index("grp")
    is_end = jnp.logical_or(me // 2 == 0, me // 2 == blocks // 2 - 1)

    def moved(value, axis, route):
        if not isinstance(value, tuple):
            return lax.ppermute(value, axis, route)
        pieces = []
        for piece in value:
            pieces.append(lax.ppermute(piece, axis, route))
        return tuple(pieces)

    def swap(value, among, by):
        return moved(value, "blk", [(b, b ^ by) for b in among])

    def spread(value, by):
        return moved(value, "grp", [(g, g ^ by) for g in range(group_size)])

    def begun(value):
        return {0: value, group_size // 2: spread(value, group_size // 2)}

    def finished(arrays):
        by = group_size // 4
        while by:
            arrays = arrays | {key ^ by: spread(array, by) for key, array in arrays.items()}
            by //= 2
        return [arrays[key] for key in range(group_size)]

    def held_for(value, *after):
        return tied(value, *after)[0]

    def either(inner_value, end_value):
        return jnp.where(is_end, end_value, inner_value)

    groups = [mine ^ j for j in range(group_size)]

    def planned(units, served=()):
        choice, slots = list(served), [me * 0, me * 0 + 1][: len(served)]
        for inner_half, end_half in units:
            choice.append(either(*(2 * c + h for c, h, _ in (inner_half, end_half))))
            slots.append(either(*(2 * (me ^ slot) + h for _, h, slot in (inner_half, end_half))))
        return plan_of(choice, slots, groups)

    def put(out, columns, plan):
        halves = [half for column in columns for half in column]
        return products(out, [rows], halves, plan, blocks, scale_coef)[0]

    def both(inner_column, inner_slot, end_column, end_slot):
        return [((inner_column, h, inner_slot), (end_column, h, end_slot)) for h in (0, 1)]

    whole, *own = laid_out(spectra[0], detector_valid[0], 2)
    own = tuple(own)
    near = swap(own, devices, 2)
    beside = swap(own, devices, 1)
    across = swap(own, inner, 6)
    rows = begun(whole)
    last = group_size // 2
    rows[last] = held_for(rows[last], *near, *beside, *across)
    rows = [(array,) for array in finished(rows)]

    far_end = swap(near, inner, 6)
    end_beside = swap(beside, ends, 2)
    far_inner = swap(across, inner, 2)
    across_beside = swap(across, inner, 1)
    near_beside = swap(near, ends, 1)
    client = begun(near)

    zero, one = me * 0, me * 0 + 1
    units_c = both(0, 7, 3, 6) + [((1, 1, 4), (3, 1, 4)), ((2, 1, 3), (4, 1, 3))]
    plan_c = planned(units_c, [zero + 2, zero + 3])
    plans = [
        planned(both(0, 0, 0, 0) + both(1, 2, 1, 2) + both(2, 1, 2, 1) + both(3, 6, 0, 5)),
        planned([((0, 0, 4), (2, 0, 4)), ((1, 0, 3), (3, 0, 3))]),
        plan_c,
        planned(both(0, 5, 1, 5)),
        plan_of([zero, one], [zero, one], groups),
    ]
    plan_a, plan_b, plan_c, plan_d, plan_served = passed(plans)
    out = put(
        None,
        [own, near, beside, across],
        plan_a,
    )
    *held, first_out = tied(far_end[0], far_inner[0], client[last][0], out)
    low = swap(held[0], inner, 1)
    low_beside = swap(held[1], ends, 1)
    firsts = finished({0: near[0], last: held[2]})
    out = put(
        first_out,
        [far_end[:1] * 2, end_beside[:1] * 2, far_inner[:1] * 2, near_beside[:1] * 2],
        plan_b,
    )
    *held, out = tied(end_beside[1], across_beside[1], client[last][1], out)
    high = swap(held[0], inner, 6)
    high_beside = swap(held[1], inner, 2)
    seconds = finished({0: near[1], last: held[2]})
    client = list(zip(firsts, seconds))

    def deliver(block, unit_size):
        block = swap(block.astype(jnp.float16), inner, 2)
        return block, swap(unit_size, inner, 2)

    def place(out, sent, end_slot):
        block, unit_size = sent
        block = block.astype(jnp.float32) * unit_size[None, :, :1, :1]
        start = (me ^ end_slot) * shard_rows
        starts = [jnp.zeros_like(start)] * 3 + [start]
        kept = lax.dynamic_slice(out, starts, block.shape)
        return lax.dynamic_update_slice(out, jnp.where(is_end, block, kept), starts)

    columns = [across_beside, far_end, end_beside, far_inner, near_beside]
    out, *first = products(
        out,
        [rows, client],
        [half for column in columns for half in column],
        plan_c,
        blocks,
        scale_coef,
        served=1,
    )
    sent_a = deliver(*first)
    low, high, out = tied(low, high, out)
    second = products(None, [client], [low, high], plan_served, blocks, scale_coef, served=1)
    sent_b = deliver(*second)
    out, _ = tied(out, second[1])
    out = put(out, [(low, high), (low_beside, high_beside)], plan_d)
    out = place(out, sent_a, 6)
    out = place(out, sent_b, 7)
    return out.reshape(shape)


def solution(mesh):
    return jax.shard_map(
        shards,
        mesh=mesh,
        in_specs=(P("grp", "blk", None, None, None), P("grp", "blk")),
        out_specs=P(None, None, "blk", "grp"),
        check_vma=False,
    )
```

```python
import functools
import math

import jax
import jax.numpy as jnp
from jax import lax
from jax.experimental import pallas as pl
from jax.experimental.pallas import tpu as pltpu
from jax.sharding import PartitionSpec as P


NT = (((1,), (1,)), ((), ()))
LANES = 128
FLOOR = 1e-30


def tile_of(size, most):
    tile = 1
    while tile * 2 <= most and size % (tile * 2) == 0:
        tile *= 2
    return tile


def passed_body(count, *refs):
    for value_ref, out_ref in zip(refs[:count], refs[count:]):
        out_ref[...] = value_ref[...]


def passed(values):
    return pl.pallas_call(
        functools.partial(passed_body, len(values)),
        out_shape=[jax.ShapeDtypeStruct(value.shape, value.dtype) for value in values],
    )(*values)


def tied(*values):
    return lax.optimization_barrier(values)


def split_in_three(value):
    parts = []
    for _ in range(2):
        part = value.astype(jnp.bfloat16).astype(jnp.float32)
        parts.append(part)
        value = value - part
    return parts + [value]


def laid_out_body(per_piece, spectra_ref, flags_ref, whole_ref, *refs):
    *piece_refs, flag_rows = refs
    high, parts, bins, taps = spectra_ref.shape
    half_width = bins * taps

    @pl.when(pl.program_id(0) == 0)
    def _():
        flags = flags_ref[...].astype(jnp.float32)
        flag_rows[...] = jnp.broadcast_to(flags, (LANES, flags.shape[1])).T

    def fill(out_ref):
        power = jnp.zeros((high, 1), jnp.float32)
        for part in range(parts):
            flat = spectra_ref[:, part].reshape(high, half_width)
            out_ref[:, part * half_width : (part + 1) * half_width] = flat
            widened = flat.astype(jnp.float32)
            power = power + jnp.sum(widened * widened, axis=1, keepdims=True)
        power_mean = power / (parts * half_width)
        here = pl.ds(pl.multiple_of(pl.program_id(0) * high, high), high)
        factor = flag_rows[here, 0:1] * lax.rsqrt(power_mean + 1e-06)
        norm = lax.rsqrt(jnp.maximum(power_mean, FLOOR))
        lane = lax.broadcasted_iota(jnp.int32, (high, LANES), 1)
        marks = jnp.zeros((high, LANES), jnp.float32)
        for index, value in enumerate(split_in_three(factor) + split_in_three(norm)):
            marks = jnp.where(lane == index, value, marks)
        out_ref[:, parts * half_width :] = marks.astype(jnp.bfloat16)

    fill(whole_ref)
    for piece, out_ref in enumerate(piece_refs):

        @pl.when(pl.program_id(0) // per_piece == piece)
        def _():
            out_ref[...] = whole_ref[...]


def laid_out(spectra, flags, pieces):
    rows, parts, bins, taps = spectra.shape
    width = parts * bins * taps + LANES
    high = tile_of(rows // pieces, 64)
    per_piece = rows // pieces // high

    def place(piece):
        first = piece * per_piece
        return lambda i: (jnp.clip(i - first, 0, per_piece - 1), 0)

    return pl.pallas_call(
        functools.partial(laid_out_body, per_piece),
        grid=(rows // high,),
        in_specs=[
            pl.BlockSpec((high, parts, bins, taps), lambda i: (i, 0, 0, 0)),
            pl.BlockSpec((1, rows), lambda i: (0, 0)),
        ],
        scratch_shapes=[pltpu.VMEM((rows, LANES), jnp.float32)],
        out_specs=[pl.BlockSpec((high, width), lambda i: (i, 0))]
        + [pl.BlockSpec((high, width), place(piece)) for piece in range(pieces)],
        out_shape=[jax.ShapeDtypeStruct((rows, width), spectra.dtype)]
        + [jax.ShapeDtypeStruct((rows // pieces, width), spectra.dtype)] * pieces,
    )(spectra, flags.reshape(1, rows))


def products_body(sizes, scale_coef, plan_ref, *refs):
    sets, at_once, known, units, served, given = sizes
    refs = list(refs)
    row_sets, at = [], 0
    for shapes in sets:
        rows = []
        for shape in shapes:
            rows.append(refs[at : at + len(shape)])
            at += len(shape)
        row_sets.append(rows)
    columns = refs[at : at + known]
    held, right, col_marks, staged, inverse, row_sems, col_sems, out_sems = refs[-8:]
    main = [] if served == units else [refs[at + known + given]]
    extra = refs[-10:-8] if served else []
    unit, part = pl.program_id(0), pl.program_id(1)
    parts = len(row_sets[0]) // at_once
    now = unit * parts + part
    shard_rows = held.shape[1] // at_once
    cols, half_width = right.shape[1] // 2, right.shape[2] // 2
    half_cols = cols // 2

    def for_set(which_unit, body):
        if len(row_sets) == 1:
            body(row_sets[0])
        else:
            pl.when(which_unit < served)(lambda: body(row_sets[1]))
            pl.when(which_unit >= served)(lambda: body(row_sets[0]))

    def row_copies(pieces, row, slot):
        copies, top = [], row * shard_rows
        for number, piece in enumerate(pieces):
            where = held.at[slot, pl.ds(top, piece.shape[0])]
            copies.append(pltpu.make_async_copy(piece, where, row_sems.at[slot, row, number]))
            top += piece.shape[0]
        return copies

    def start_rows(which_unit, which, slot):
        def start(rows):
            for index in range(parts):

                @pl.when(which == index)
                def _():
                    for row in range(at_once):
                        for copy in row_copies(rows[index * at_once + row], row, slot):
                            copy.start()

        for_set(which_unit, start)

    def wait_rows(rows):
        for row in range(at_once):
            for copy in row_copies(rows[row], row, slot):
                copy.wait()

    def col_copies(source, half, slot):
        top = half * half_cols
        real = source.at[:, pl.ds(0, half_width)]
        imag = source.at[:, pl.ds(half_width, half_width)]
        marks = source.at[:, pl.ds(2 * half_width, LANES)]
        places = [
            (real, right.at[slot, pl.ds(top, half_cols), pl.ds(0, half_width)]),
            (imag, right.at[slot, pl.ds(top, half_cols), pl.ds(half_width, half_width)]),
            (real, right.at[slot, pl.ds(cols + top, half_cols), pl.ds(half_width, half_width)]),
            (marks, col_marks.at[slot, pl.ds(top, half_cols)]),
        ]
        return [
            pltpu.make_async_copy(start, end, col_sems.at[slot, half, kind])
            for kind, (start, end) in enumerate(places)
        ]

    def start_cols(which, slot):
        for half in range(2):
            for index in range(known):

                @pl.when(plan_ref[2 * which + half] == index)
                def _():
                    for copy in col_copies(columns[index], half, slot):
                        copy.start()

    def out_copies(slot, target_ref=None):
        target_ref = (main + extra)[0] if target_ref is None else target_ref
        copies = []
        for row in range(at_once):
            group = plan_ref[4 * units + part * at_once + row]
            for half in range(2):
                start = plan_ref[2 * units + 2 * unit + half] * half_cols
                lanes = pl.ds(pl.multiple_of(start, half_cols), half_cols)
                source = staged.at[slot, :, row, :, pl.ds(half * half_cols, half_cols)]
                target = target_ref.at[:, group, :, lanes]
                copies.append(pltpu.make_async_copy(source, target, out_sems.at[slot, row, half]))
        return copies

    slot, col_slot = lax.rem(now, 2), lax.rem(unit, 2)

    @pl.when(now == 0)
    def _():
        start_rows(0, 0, 0)
        start_cols(0, 0)

    @pl.when(now + 1 < units * parts)
    def _():
        start_rows(lax.div(now + 1, parts), lax.rem(part + 1, parts), lax.rem(now + 1, 2))

    @pl.when(jnp.logical_and(part == 0, unit + 1 < units))
    def _():
        start_cols(unit + 1, lax.rem(unit + 1, 2))

    @pl.when(part == 0)
    def _():
        for half in range(2):
            for copy in col_copies(columns[0], half, col_slot):
                copy.wait()
        right[col_slot, cols:, :half_width] = -right[col_slot, :cols, half_width:]

    for_set(unit, wait_rows)
    left = held[slot, :, : 2 * half_width]
    product = lax.dot_general(left, right[col_slot], NT, preferred_element_type=jnp.float32)

    @pl.when(now >= 2)
    def _():
        for copy in out_copies(slot):
            copy.wait()

    def sums(values, axis):
        def one(first):
            take = [lax.slice_in_dim(values, i, i + 1, axis=axis) for i in range(first, first + 3)]
            return (take[2] + take[1]) + take[0]

        return one(0), one(3)

    col_factor, col_norm = sums(col_marks[col_slot].astype(jnp.float32).T, 0)
    for row in range(at_once):
        top = row * shard_rows
        marks = held[slot, pl.ds(top, shard_rows), pl.ds(2 * half_width, LANES)]
        row_factor, row_norm = sums(marks.astype(jnp.float32), 1)
        scaling = (row_factor * scale_coef) * col_factor
        if served:

            @pl.when(unit < served)
            def _():
                bound = jnp.max(row_factor / row_norm, axis=0, keepdims=True)
                bound = bound * jnp.max(col_factor / col_norm, axis=1, keepdims=True)
                unit_size = jnp.maximum(bound * (2 * half_width * scale_coef), FLOOR) / 32768
                group = plan_ref[4 * units + part * at_once + row]
                extra[1][group] = jnp.broadcast_to(unit_size, extra[1].shape[1:])
                inverse[...] = jnp.broadcast_to(1 / unit_size, inverse.shape)

            if main:

                @pl.when(unit >= served)
                def _():
                    inverse[...] = jnp.ones_like(inverse)

            scaling = scaling * inverse[0:1, 0:1]
        staged[slot, 0, row] = product[top : top + shard_rows, :cols] * scaling
        staged[slot, 1, row] = product[top : top + shard_rows, cols:] * scaling

    def start_out(target_ref):
        for copy in out_copies(slot, target_ref):
            copy.start()

    if served and main:
        pl.when(unit < served)(lambda: start_out(extra[0]))
        pl.when(unit >= served)(lambda: start_out(main[0]))
    else:
        start_out((main + extra)[0])

    @pl.when(now == units * parts - 1)
    def _():
        for copy in out_copies(lax.rem(now + 1, 2)) + out_copies(slot):
            copy.wait()


def plan_of(choice, slots, groups):
    return jnp.stack(list(choice) + list(slots) + list(groups)).astype(jnp.int32)


def products(out, row_sets, columns, plan, blocks, scale_coef, served=0):
    count = len(row_sets[0])
    units = (plan.shape[0] - count) // 4
    shard_rows = sum(piece.shape[0] for piece in row_sets[0][0])
    width = row_sets[0][0][0].shape[1]
    kind = row_sets[0][0][0].dtype
    half_width = (width - LANES) // 2
    at_once = 2 if units > 1 and count > 1 else 1
    parts = count // at_once
    cols = 2 * columns[0].shape[0]
    whole = pl.BlockSpec(memory_space=pl.ANY)
    operands = [piece for rows in row_sets for pieces in rows for piece in pieces]
    operands += list(columns)
    aliases = {}
    if out is not None:
        aliases = {1 + len(operands): 0}
        operands.append(out)
    out_shape, out_specs = [], []
    if served < units:
        shape = (2, count, shard_rows, shard_rows * blocks)
        out_shape.append(jax.ShapeDtypeStruct(shape, jnp.float32))
        out_specs.append(whole)
    if served:
        sizes = (count, 8, LANES)
        out_shape.append(jax.ShapeDtypeStruct((2, count, shard_rows, cols), jnp.float32))
        out_shape.append(jax.ShapeDtypeStruct(sizes, jnp.float32))
        out_specs += [whole, pl.BlockSpec(sizes, lambda i, j, s: (0, 0, 0))]
    sets = [[[piece.shape[0] for piece in pieces] for pieces in rows] for rows in row_sets]
    most = max(len(pieces) for rows in row_sets for pieces in rows)
    sizes = (sets, at_once, len(columns), units, served, int(out is not None))
    return pl.pallas_call(
        functools.partial(products_body, sizes, scale_coef),
        grid_spec=pltpu.PrefetchScalarGridSpec(
            num_scalar_prefetch=1,
            grid=(units, parts),
            in_specs=[whole] * len(operands),
            out_specs=out_specs,
            scratch_shapes=[
                pltpu.VMEM((2, at_once * shard_rows, width), kind),
                pltpu.VMEM((2, 2 * cols, 2 * half_width), kind),
                pltpu.VMEM((2, cols, LANES), kind),
                pltpu.VMEM((2, 2, at_once, shard_rows, cols), jnp.float32),
                pltpu.VMEM((8, LANES), jnp.float32),
                pltpu.SemaphoreType.DMA((2, at_once, most)),
                pltpu.SemaphoreType.DMA((2, 2, 4)),
                pltpu.SemaphoreType.DMA((2, at_once, 2)),
            ],
        ),
        out_shape=out_shape,
        input_output_aliases=aliases,
        cost_estimate=pl.CostEstimate(
            flops=8 * units * count * shard_rows * cols * half_width,
            bytes_accessed=4 * units * half_width * (count * shard_rows + cols),
            transcendentals=0,
        ),
        compiler_params=pltpu.CompilerParams(
            dimension_semantics=("arbitrary", "arbitrary"), vmem_limit_bytes=60 * 2**20
        ),
    )(plan, *operands)


def gathered(spectra, detector_valid, scale_coef):
    shard_rows = spectra.shape[1]
    half_width = spectra.shape[3] * spectra.shape[4]
    flattened = spectra.reshape(shard_rows, 2 * half_width)
    widened = flattened.astype(jnp.float32)
    power_mean = jnp.mean(widened * widened, axis=1) + 1e-06
    own_factor = detector_valid.reshape(shard_rows).astype(jnp.float32) * lax.rsqrt(power_mean)
    rows = lax.all_gather(flattened, "grp", axis=0, tiled=True)
    cols = lax.all_gather(flattened, "blk", axis=0, tiled=True)
    row_factor = lax.all_gather(own_factor, "grp", axis=0, tiled=True) * scale_coef
    col_factor = lax.all_gather(own_factor, "blk", axis=0, tiled=True)
    rotated = jnp.concatenate([-cols[:, half_width:], cols[:, :half_width]], axis=1)
    scaling = row_factor[:, None] * col_factor[None, :]
    parts = [
        lax.dot_general(rows, right, NT, preferred_element_type=jnp.float32) * scaling
        for right in (cols, rotated)
    ]
    return jnp.stack(parts)


def shards(spectra, detector_valid):
    shard_rows = spectra.shape[1]
    half_width = spectra.shape[3] * spectra.shape[4]
    blocks = lax.axis_size("blk")
    group_size = lax.axis_size("grp")
    scale_coef = 0.5 / math.sqrt(half_width)
    shape = (2, group_size, shard_rows, blocks * shard_rows)
    fits = shard_rows % 256 == 0 and half_width % 128 == 0 and group_size & (group_size - 1) == 0
    if blocks != 8 or group_size < 2 or not fits:
        return gathered(spectra, detector_valid, scale_coef).reshape(shape)

    devices = range(blocks)
    inner = [b for b in devices if 0 < b // 2 < blocks // 2 - 1]
    ends = [b for b in devices if b not in inner]
    me = lax.axis_index("blk")
    mine = lax.axis_index("grp")
    is_end = jnp.logical_or(me // 2 == 0, me // 2 == blocks // 2 - 1)

    def moved(value, axis, route):
        if not isinstance(value, tuple):
            return lax.ppermute(value, axis, route)
        pieces = []
        for piece in value:
            pieces.append(lax.ppermute(piece, axis, route))
        return tuple(pieces)

    def swap(value, among, by):
        return moved(value, "blk", [(b, b ^ by) for b in among])

    def spread(value, by):
        return moved(value, "grp", [(g, g ^ by) for g in range(group_size)])

    def begun(value):
        return {0: value, group_size // 2: spread(value, group_size // 2)}

    def finished(arrays):
        by = group_size // 4
        while by:
            arrays = arrays | {key ^ by: spread(array, by) for key, array in arrays.items()}
            by //= 2
        return [arrays[key] for key in range(group_size)]

    def held_for(value, *after):
        return tied(value, *after)[0]

    def either(inner_value, end_value):
        return jnp.where(is_end, end_value, inner_value)

    groups = [mine ^ j for j in range(group_size)]

    def planned(units, served=()):
        choice, slots = list(served), [me * 0, me * 0 + 1][: len(served)]
        for inner_half, end_half in units:
            choice.append(either(*(2 * c + h for c, h, _ in (inner_half, end_half))))
            slots.append(either(*(2 * (me ^ slot) + h for _, h, slot in (inner_half, end_half))))
        return plan_of(choice, slots, groups)

    def put(out, columns, plan):
        halves = [half for column in columns for half in column]
        return products(out, [rows], halves, plan, blocks, scale_coef)[0]

    def both(inner_column, inner_slot, end_column, end_slot):
        return [((inner_column, h, inner_slot), (end_column, h, end_slot)) for h in (0, 1)]

    whole, *own = laid_out(spectra[0], detector_valid[0], 2)
    own = tuple(own)
    near = swap(own, devices, 2)
    beside = swap(own, devices, 1)
    across = swap(own, inner, 6)
    rows = begun(whole)
    last = group_size // 2
    rows[last] = held_for(rows[last], *near, *beside, *across)
    rows = [(array,) for array in finished(rows)]

    far_end = swap(near, inner, 6)
    end_beside = swap(beside, ends, 2)
    far_inner = swap(across, inner, 2)
    across_beside = swap(across, inner, 1)
    near_beside = swap(near, ends, 1)
    client = begun(near)

    zero, one = me * 0, me * 0 + 1
    units_c = both(0, 7, 3, 6) + [((1, 1, 4), (3, 1, 4)), ((2, 1, 3), (4, 1, 3))]
    plan_c = planned(units_c, [zero + 2, zero + 3])
    plans = [
        planned(both(0, 0, 0, 0) + both(1, 2, 1, 2) + both(2, 1, 2, 1) + both(3, 6, 0, 5)),
        planned([((0, 0, 4), (2, 0, 4)), ((1, 0, 3), (3, 0, 3))]),
        plan_c,
        planned(both(0, 5, 1, 5)),
        plan_of([zero, one], [zero, one], groups),
    ]
    plan_a, plan_b, plan_c, plan_d, plan_served = passed(plans)
    out = put(
        None,
        [own, near, beside, across],
        plan_a,
    )
    *held, first_out = tied(far_end[0], far_inner[0], client[last][0], out)
    low = swap(held[0], inner, 1)
    low_beside = swap(held[1], ends, 1)
    firsts = finished({0: near[0], last: held[2]})
    out = put(
        first_out,
        [far_end[:1] * 2, end_beside[:1] * 2, far_inner[:1] * 2, near_beside[:1] * 2],
        plan_b,
    )
    *held, out = tied(end_beside[1], across_beside[1], client[last][1], out)
    high = swap(held[0], inner, 6)
    high_beside = swap(held[1], inner, 2)
    seconds = finished({0: near[1], last: held[2]})
    client = list(zip(firsts, seconds))

    def deliver(block, unit_size):
        block = swap(block.astype(jnp.float16), inner, 2)
        return block, swap(unit_size, inner, 2)

    def place(out, sent, end_slot):
        block, unit_size = sent
        block = block.astype(jnp.float32) * unit_size[None, :, :1, :1]
        start = (me ^ end_slot) * shard_rows
        starts = [jnp.zeros_like(start)] * 3 + [start]
        kept = lax.dynamic_slice(out, starts, block.shape)
        return lax.dynamic_update_slice(out, jnp.where(is_end, block, kept), starts)

    columns = [across_beside, far_end, end_beside, far_inner, near_beside]
    out, *first = products(
        out,
        [rows, client],
        [half for column in columns for half in column],
        plan_c,
        blocks,
        scale_coef,
        served=1,
    )
    sent_a = deliver(*first)
    low, high, out = tied(low, high, out)
    second = products(None, [client], [low, high], plan_served, blocks, scale_coef, served=1)
    sent_b = deliver(*second)
    out, _ = tied(out, second[1])
    out = put(out, [(low, high), (low_beside, high_beside)], plan_d)
    out = place(out, sent_a, 6)
    out = place(out, sent_b, 7)
    return out.reshape(shape)


def solution(mesh):
    return jax.shard_map(
        shards,
        mesh=mesh,
        in_specs=(P("grp", "blk", None, None, None), P("grp", "blk")),
        out_specs=P(None, None, "blk", "grp"),
        check_vma=False,
    )
```
